32 devices in a mesh: seq: 8 (over z, y), fsdp: 4 (over x, core).
Axes of the slice: x: 2, y: 2, z: 4, core: 2. Of those that a mesh axis runs over, the one named last changes fastest.
Arguments:
- conv_input: bfloat16 [4096, 4096], P('seq', 'fsdp'), may hold values from -6 to 6
- gate: bfloat16 [4096, 4096], P('seq', 'fsdp'), may hold values from -6 to 6
- out_grad: bfloat16 [4096, 4096], P('seq', 'fsdp'), may hold values from -16 to 16
- filters: float32 [256, 128], P(None, 'fsdp'), may hold values from -0.8 to 0.8
- skip_bias: float32 [4096], P('fsdp'), may hold values from -5 to 5
Outputs:
- input_grad: bfloat16 [4096, 4096], P('seq', 'fsdp')
- filter_grad: float32 [256, 128], P(None, 'fsdp')
- bias_grad: float32 [4096], P('fsdp')
The draws below stay inside these ranges and needn't reach their ends.
All inputs are finite; a program needn't handle non-finite values.
Results may differ from the reference program's by a relative error of at most 0.0056.
Values may be sent and summed in bfloat16 or wider, within the bound.
A program may use at most 128 MiB of HBM per device.

```python
import jax
import jax.numpy as jnp
from jax import lax

C = 4096
GS = 16
LF = 128
G = 256
SEQUENCE_TOKENS = 4096


def draw_out_grad(key, part):
    position = jnp.arange(SEQUENCE_TOKENS, dtype=jnp.float32)[:, None] / SEQUENCE_TOKENS
    base = jnp.clip(jax.random.normal(key, (SEQUENCE_TOKENS, C), jnp.float32), -5.0, 5.0)
    ramp = 1.0 + 2.0 * position
    return (base * ramp).astype(jnp.bfloat16)


def draw_filters(key, part):
    first_key, second_key = jax.random.split(key)
    lag = jnp.arange(LF, dtype=jnp.float32)[None, :]
    values = jnp.clip(jax.random.normal(first_key, (G, LF), jnp.float32), -4.0, 4.0)
    length = jnp.exp(jax.random.uniform(second_key, (G, 1), jnp.float32, jnp.log(20.0), jnp.log(2000.0)))
    return 0.2 * values * jnp.exp(-lag / length)


def steps_of(stream_key, shape, shards, smallest, high):
    gain, own = 1.0, jax.random.fold_in(stream_key, 6)
    for axis_at, parts in shards:
        heights = jnp.exp(jax.random.uniform(jax.random.fold_in(own, axis_at), (parts,), jnp.float32, smallest / len(shards), high / len(shards)))
        gain = gain * jnp.repeat(heights, shape[axis_at] // parts).reshape([-1 if axis == axis_at else 1 for axis in range(len(shape))])
    return gain


def bell_draw(key, shape, spread, limit, shards=(), held_as=jnp.bfloat16):
    drawn = jax.random.normal(key, shape, jnp.float32) * spread
    if len(shards) > 0:
        drawn = steps_of(key, shape, shards, -0.22, 0.18) * drawn
    return jnp.clip(drawn, min=-limit, max=limit).astype(held_as)


def setup_inputs(seed: int = 0) -> dict:
    key_of = jax.random.split(jax.random.key(seed), 6)
    return {
        "conv_input": bell_draw(key_of[0], (SEQUENCE_TOKENS, C), 1.0, 6.0, ((0, 8), (1, 4))),
        "gate": bell_draw(key_of[1], (SEQUENCE_TOKENS, C), 1.0, 6.0, ((0, 8), (1, 4))),
        "out_grad": draw_out_grad(jax.random.fold_in(key_of[5], 71), 0),
        "filters": draw_filters(jax.random.fold_in(key_of[5], 71), 0),
        "skip_bias": bell_draw(key_of[4], (C,), 1.0, 5.0, ((0, 4),), jnp.float32),
    }


def reference(conv_input, gate, out_grad, filters, skip_bias):
    row_count = conv_input.shape[0]
    chan_count = conv_input.shape[1]
    scaled_grad = (out_grad.astype(jnp.float32) * gate.astype(jnp.float32)).astype(jnp.bfloat16)
    filter_copy = lax.optimization_barrier(filters.astype(jnp.bfloat16)).astype(jnp.float32)
    grad_float = scaled_grad.astype(jnp.float32)
    input_float = conv_input.astype(jnp.float32)
    padded_input = jnp.concatenate([grad_float, jnp.zeros((LF, chan_count), jnp.float32)], axis=0)
    channel_taps = jnp.repeat(filter_copy, GS, axis=0)

    def one_tap(total, lag):
        moved = lax.dynamic_slice_in_dim(padded_input, lag, row_count, 0)
        weight = lax.dynamic_slice_in_dim(channel_taps, lag, 1, 1)[:, 0]
        return total + moved * weight[None, :], jnp.sum(moved * input_float, axis=0)

    convolved, columns = lax.scan(one_tap, jnp.zeros((row_count, chan_count), jnp.float32),
                                  jnp.arange(LF, dtype=jnp.int32))
    input_grad = (convolved + skip_bias[None, :] * grad_float).astype(jnp.bfloat16)
    filter_grad = jnp.sum(columns.reshape(LF, chan_count // GS, GS), axis=2).T
    bias_grad = jnp.sum(grad_float * input_float, axis=0)
    return input_grad, filter_grad, bias_grad
```

```python
import functools

import jax
import jax.numpy as jnp
from jax import lax
from jax.experimental import pallas as pl
from jax.experimental.pallas import tpu as pltpu
from jax.sharding import PartitionSpec as P

GS = 16
VMEM_GRANT = 105 << 19
LF = 128
LANES = 128
PER = LANES // GS
MESH = pl.DeviceIdType.MESH
F32 = jnp.float32
BF16 = jnp.bfloat16


def kernel(
    seq_size, fsdp_size, fused,
    x_hbm, gate_hbm, og_hbm, filt_hbm, skip_hbm,
    ig_hbm, fg_ref, bias_ref,
    skip_ref, x_v, gate_v, og_v, sg_v, out_v, toep_v, taps_r, taps_v, acc_v, part_v, bias_v,
    bias_r, p1_r, tile_v, p2_r,
    load_sem, out_sem, halo_send, halo_recv, tap_send, tap_recv, bias_send, bias_recv,
    p1_send, p1_recv, p2_send, p2_recv,
):
    rows, chans = x_v.shape
    blocks = chans // LANES
    pairs = rows // (2 * LF)
    groups = chans // GS
    me_s = lax.axis_index("seq")
    me_f = lax.axis_index("fsdp")

    width = LF // fsdp_size
    sharing = LANES // groups

    def tap_lanes(owner):
        return pl.ds(pl.multiple_of(lax.div(owner, sharing) * LANES, LANES), LANES)

    def tap_rows(source):
        return pl.ds(pl.multiple_of(source * width, 8), width)

    rim = pl.ds(0, LF)
    rest = pl.ds(LF, rows - LF)
    loads = [
        pltpu.make_async_copy(og_hbm.at[rim], og_v.at[rim], load_sem.at[0]),
        pltpu.make_async_copy(gate_hbm.at[rim], gate_v.at[rim], load_sem.at[1]),
        pltpu.make_async_copy(og_hbm.at[rest], og_v.at[rest], load_sem.at[2]),
        pltpu.make_async_copy(gate_hbm.at[rest], gate_v.at[rest], load_sem.at[3]),
        pltpu.make_async_copy(x_hbm, x_v, load_sem.at[4]),
        pltpu.make_async_copy(
            filt_hbm.at[:, tap_lanes(me_f)], taps_r.at[tap_rows(me_f)], load_sem.at[5]),
        pltpu.make_async_copy(skip_hbm, skip_ref, load_sem.at[6]),
    ]
    for load in loads:
        load.start()

    barrier = pltpu.get_barrier_semaphore()
    if fused:
        total = seq_size * fsdp_size
        me = me_s * fsdp_size + me_f

        def greet(i, c):
            other = lax.rem(me + i, total)
            pl.semaphore_signal(
                barrier, inc=1,
                device_id=(lax.div(other, fsdp_size), lax.rem(other, fsdp_size)),
                device_id_type=MESH)
            return c

        lax.fori_loop(1, total, greet, 0)
    else:
        for d in range(1, fsdp_size):
            pl.semaphore_signal(
                barrier, inc=1, device_id=(me_s, lax.rem(me_f + d, fsdp_size)),
                device_id_type=MESH)

        @pl.when(me_s > 0)
        def _():
            pl.semaphore_signal(
                barrier, inc=1, device_id=(me_s - 1, me_f), device_id_type=MESH)

        @pl.when(me_s < seq_size - 1)
        def _():
            pl.semaphore_signal(
                barrier, inc=1, device_id=(me_s + 1, me_f), device_id_type=MESH)

    loads[0].wait()
    loads[1].wait()
    sg_v[rim, :] = (og_v[rim, :].astype(F32) * gate_v[rim, :].astype(F32)).astype(BF16)

    if fused:
        pl.semaphore_wait(barrier, total - 1)
    else:
        pl.semaphore_wait(barrier, fsdp_size - 1)

        @pl.when(me_s > 0)
        def _():
            pl.semaphore_wait(barrier, 1)

        @pl.when(me_s < seq_size - 1)
        def _():
            pl.semaphore_wait(barrier, 1)

    def tap_copy(d):
        other = lax.rem(me_f + d, fsdp_size)
        return pltpu.make_async_remote_copy(
            src_ref=filt_hbm.at[:, tap_lanes(other)],
            dst_ref=taps_r.at[tap_rows(me_f)],
            send_sem=tap_send.at[other], recv_sem=tap_recv.at[me_f],
            device_id=(me_s, other), device_id_type=MESH)

    def tap_arrival(d):
        other = lax.rem(me_f + d, fsdp_size)
        return pltpu.make_async_remote_copy(
            src_ref=filt_hbm.at[:, tap_lanes(other)],
            dst_ref=taps_r.at[tap_rows(other)],
            send_sem=tap_send.at[other], recv_sem=tap_recv.at[other],
            device_id=(me_s, other), device_id_type=MESH)

    for d in range(1, fsdp_size):
        tap_copy(d).start()

    def lanes_of(b):
        return pl.ds(pl.multiple_of(b * LANES, LANES), LANES)

    def halo_copy(target, b):
        return pltpu.make_async_remote_copy(
            src_ref=sg_v.at[rim, lanes_of(b)], dst_ref=sg_v.at[pl.ds(rows, LF), lanes_of(b)],
            send_sem=halo_send.at[b], recv_sem=halo_recv.at[b],
            device_id=(target, me_f), device_id_type=MESH)

    def each_block(do):
        def step(b, c):
            do(b)
            return c
        lax.fori_loop(0, blocks, step, 0)

    @pl.when(me_s > 0)
    def _():
        each_block(lambda b: halo_copy(me_s - 1, b).start())

    @pl.when(me_s == seq_size - 1)
    def _():
        sg_v[pl.ds(rows, LF), :] = jnp.zeros((LF, chans), BF16)

    for load in loads[2:5]:
        load.wait()

    def scale(b, c):
        lanes = lanes_of(b)
        new = (og_v[rest, lanes].astype(F32) * gate_v[rest, lanes].astype(F32)).astype(BF16)
        sg_v[rest, lanes] = new
        terms = jnp.sum(new.astype(F32) * x_v[rest, lanes].astype(F32), axis=0, keepdims=True)
        terms = terms + jnp.sum(
            sg_v[rim, lanes].astype(F32) * x_v[rim, lanes].astype(F32), axis=0, keepdims=True)
        bias_v[pl.ds(b, 1), :] = terms
        return c

    lax.fori_loop(0, blocks, scale, 0, unroll=2)

    if fused:
        def bias_copy(d, slot):
            other = lax.rem(me_s + d, seq_size)
            return pltpu.make_async_remote_copy(
                src_ref=bias_v, dst_ref=bias_r.at[me_s if slot is None else other],
                send_sem=bias_send.at[other],
                recv_sem=bias_recv.at[me_s if slot is None else other],
                device_id=(other, me_f), device_id_type=MESH)

        for d in range(1, seq_size):
            bias_copy(d, None).start()

    row_at = lax.broadcasted_iota(jnp.int32, (LF, LANES), 0)
    lane_at = lax.broadcasted_iota(jnp.int32, (LF, LANES), 1)
    above = lane_at >= row_at

    def windows(p, lanes):
        at = 2 * LF * p
        return jnp.concatenate(
            [sg_v[at:at + 2 * LF, lanes], sg_v[at + LF:at + 3 * LF, lanes]], axis=1)

    def split_groups(both):
        lane = lax.broadcasted_iota(jnp.int32, both.shape, 1)
        owner = lax.rem(lax.div(lane, GS), PER)
        return jnp.concatenate(
            [both * (owner == g).astype(F32).astype(BF16) for g in range(PER)], axis=0)

    def products(left, right):
        return lax.dot_general(
            split_groups(left), right, (((1,), (1,)), ((), ())), preferred_element_type=F32)

    def fold(wrapped):
        total = wrapped[:8]
        for k in range(1, LF // 8):
            total = total + pltpu.roll(wrapped[8 * k:8 * k + 8], LANES - 8 * k, 1)
        return total

    def corr_early(b, c):
        lanes = lanes_of(b)
        tiles = [slice(at, at + LF) for at in range(0, rows, LF)]
        left = jnp.concatenate([x_v[tile, lanes] for tile in tiles], axis=1)
        right = jnp.concatenate(
            [sg_v[at:at + 2 * LF, lanes] for at in range(0, rows - LF, LF)]
            + [jnp.concatenate(
                [sg_v[rows - LF:rows, lanes], jnp.zeros((LF, LANES), BF16)], axis=0)], axis=1)
        prod = products(left, right)
        for g in range(PER):
            one = prod[g * LF:(g + 1) * LF]
            here = pl.ds(pl.multiple_of((b * PER + g) * 8, 8), 8)
            acc_v[here, :] = fold(jnp.where(above, one[:, :LANES], one[:, LANES:]))
        return c

    def part_copy(b, f):
        slot = me_s * fsdp_size + me_f
        return pltpu.make_async_remote_copy(
            src_ref=part_v.at[b * fsdp_size + f], dst_ref=p1_r.at[slot],
            send_sem=p1_send.at[b * fsdp_size + f], recv_sem=p1_recv.at[slot],
            device_id=(b, f), device_id_type=MESH)

    sub = lax.broadcasted_iota(jnp.int32, (8, LANES), 0)

    def corr_last(b, c):
        lanes = lanes_of(b)

        @pl.when(me_s < seq_size - 1)
        def _():
            halo_copy(me_s + 1, b).wait_recv()

        prod = products(x_v[rows - LF:rows, lanes], sg_v[rows:rows + LF, lanes])
        out = jnp.zeros((8, LANES), F32)
        for g in range(PER):
            one = prod[g * LF:(g + 1) * LF]
            at = pl.ds(pl.multiple_of((b * PER + g) * 8, 8), 8)
            whole = acc_v[at, :] + fold(jnp.where(above, jnp.zeros_like(one), one))
            for bit in range(3):
                whole = jnp.where(
                    lax.rem(lax.div(sub, 1 << bit), 2) == 1,
                    pltpu.roll(whole, LANES - (1 << bit), 1), whole)
            out = jnp.where(sub == g, jnp.sum(whole, axis=0, keepdims=True), out)
        if fused:
            for k in range(fsdp_size):
                moved = out if k == 0 else pltpu.roll(out, LANES - k * width, 1)
                part_v[b * fsdp_size + k] = moved[:, :width]

                @pl.when(b * fsdp_size + k != me)
                def _():
                    part_copy(b, k).start()
        else:
            part_v[b] = out
        return c

    def build(b, c):
        first = lax.rem(me_f, sharing) * groups + b * PER
        taps = taps_v[pl.ds(pl.multiple_of(first, PER), PER), :]
        for g in range(PER):
            band = pltpu.roll(
                jnp.broadcast_to(taps[g:g + 1], (LF, LANES)), 0, 1, stride=1, stride_axis=0)
            zero = jnp.zeros_like(band)
            toep_v[b, g * LF:(g + 1) * LF, :LANES] = jnp.where(above, band, zero).astype(BF16)
            toep_v[b, g * LF:(g + 1) * LF, LANES:] = jnp.where(above, zero, band).astype(BF16)
        return c

    def conv(b, c, p):
        lanes = lanes_of(b)
        at = 2 * LF * p
        prod = jnp.dot(toep_v[b], windows(p, lanes), preferred_element_type=F32)
        owner = lax.div(lax.broadcasted_iota(jnp.int32, (LF, 2 * LANES), 1), GS)
        owner = lax.rem(owner, PER)
        out = prod[:LF]
        for g in range(1, PER):
            out = jnp.where(owner == g, prod[g * LF:(g + 1) * LF], out)
        skip = skip_ref[pl.ds(b, 1), :]
        for half in range(2):
            here = slice(at + half * LF, at + (half + 1) * LF)
            direct = skip * sg_v[here, lanes].astype(F32)
            out_v[here, lanes] = (
                out[:, half * LANES:(half + 1) * LANES] + direct).astype(BF16)
        return c

    lax.fori_loop(0, blocks, corr_early, 0, unroll=2)

    lax.fori_loop(0, blocks, corr_last, 0, unroll=2)

    def out_copy(p):
        span = pl.ds(2 * LF * p, 2 * LF)
        return pltpu.make_async_copy(out_v.at[span], ig_hbm.at[span], out_sem.at[p])

    loads[5].wait()
    loads[6].wait()
    for d in range(1, fsdp_size):
        tap_arrival(d).wait_recv()
    taps_v[...] = taps_r[...].T
    lax.fori_loop(0, blocks, build, 0, unroll=2)

    for p in range(pairs - 1):
        lax.fori_loop(0, blocks, functools.partial(conv, p=p), 0, unroll=2)
        out_copy(p).start()

    last = functools.partial(conv, p=pairs - 1)
    if fused:
        def each_other(do):
            def step(i, c):
                other = lax.rem(me + i, total)
                do(other, lax.div(other, fsdp_size), lax.rem(other, fsdp_size))
                return c
            lax.fori_loop(1, total, step, 0)

        def part_arrived(other, o_s, o_f):
            pltpu.make_async_remote_copy(
                src_ref=part_v.at[other], dst_ref=p1_r.at[other],
                send_sem=p1_send.at[other], recv_sem=p1_recv.at[other],
                device_id=(o_s, o_f), device_id_type=MESH).wait_recv()

        def part_left(other, o_s, o_f):
            part_copy(o_s, o_f).wait_send()

        def tile_copy(d, slot):
            other = lax.rem(me_s + d, seq_size)
            at = me_s if slot is None else other
            return pltpu.make_async_remote_copy(
                src_ref=tile_v, dst_ref=p2_r.at[at],
                send_sem=p2_send.at[other], recv_sem=p2_recv.at[at],
                device_id=(other, me_f), device_id_type=MESH)

        p1_r[me] = part_v[me]
        each_other(part_arrived)
        for f in range(fsdp_size):
            piece = p1_r[f]
            for k in range(1, seq_size):
                piece = piece + p1_r[k * fsdp_size + f]
            tile_v[:, f * width:(f + 1) * width] = piece
        for d in range(1, seq_size):
            tile_copy(d, None).start()

    lax.fori_loop(0, blocks, last, 0, unroll=2)
    out_copy(pairs - 1).start()

    for d in range(1, fsdp_size):
        tap_copy(d).wait_send()

    @pl.when(me_s > 0)
    def _():
        each_block(lambda b: halo_copy(me_s - 1, b).wait_send())

    if fused:
        for d in range(1, seq_size):
            bias_copy(d, 1).wait_recv()
            bias_copy(d, 1).wait_send()
        bias_r[me_s] = bias_v[...]
        bias_total = bias_r[0]
        for k in range(1, seq_size):
            bias_total = bias_total + bias_r[k]
        bias_ref[...] = bias_total
        each_other(part_left)
        p2_r[me_s] = tile_v[...]
        for d in range(1, seq_size):
            tile_copy(d, 1).wait_recv()
            tile_copy(d, 1).wait_send()
        turned = p2_r[...].reshape(groups, LANES).T
        for f in range(fsdp_size):
            fg_ref[:, f * groups:(f + 1) * groups] = turned[f * width:(f + 1) * width]
    else:
        fg_ref[...] = part_v[...]
        bias_ref[...] = bias_v[...]
    for p in range(pairs):
        out_copy(p).wait()


def writer(*refs):
    count = len(refs) // 2
    sources, targets, sems = refs[:count], refs[count:2 * count], refs[2 * count]
    copies = [
        pltpu.make_async_copy(a, b, sems.at[i]) for i, (a, b) in enumerate(zip(sources, targets))]
    for copy in copies:
        copy.start()
    for copy in copies:
        copy.wait()


def write_out(*arrays):
    return pl.pallas_call(
        writer,
        out_shape=tuple(pltpu.HBM(a.shape, a.dtype) for a in arrays),
        in_specs=[pl.BlockSpec(memory_space=pltpu.VMEM)] * len(arrays),
        out_specs=(pl.BlockSpec(memory_space=pltpu.HBM),) * len(arrays),
        scratch_shapes=[pltpu.SemaphoreType.DMA((len(arrays),))],
    )(*(pltpu.with_memory_space_constraint(a, pltpu.VMEM) for a in arrays))


def on_device(seq_size, fsdp_size, conv_input, gate, out_grad, filters, skip_bias):
    rows, chans = conv_input.shape
    blocks = chans // LANES
    groups = chans // GS
    width = LF // fsdp_size
    fused = seq_size == blocks
    peers = seq_size if fused else 1
    everyone = seq_size * fsdp_size if fused else 1
    fg_shape = (width, fsdp_size * groups) if fused else (blocks, PER, LF)
    part_shape = (everyone, PER, width) if fused else (blocks, PER, LANES)
    hbm_spec = pl.BlockSpec(memory_space=pltpu.HBM)
    vmem_spec = pl.BlockSpec(memory_space=pltpu.VMEM)
    dma = pltpu.SemaphoreType.DMA
    input_grad, filter_part, bias_part = pl.pallas_call(
        functools.partial(kernel, seq_size, fsdp_size, fused),
        out_shape=(
            jax.ShapeDtypeStruct((rows, chans), BF16),
            jax.ShapeDtypeStruct(fg_shape, F32),
            jax.ShapeDtypeStruct((blocks, LANES), F32),
        ),
        in_specs=[hbm_spec] * 5,
        out_specs=(hbm_spec, vmem_spec, vmem_spec),
        scratch_shapes=[
            pltpu.VMEM((blocks, LANES), F32),
            pltpu.VMEM((rows, chans), BF16),
            pltpu.VMEM((rows, chans), BF16),
            pltpu.VMEM((rows, chans), BF16),
            pltpu.VMEM((rows + LF, chans), BF16),
            pltpu.VMEM((rows, chans), BF16),
            pltpu.VMEM((blocks, PER * LF, 2 * LANES), BF16),
            pltpu.VMEM((LF, LANES), F32),
            pltpu.VMEM((LANES, LF), F32),
            pltpu.VMEM((groups * 8, LANES), F32),
            pltpu.VMEM(part_shape, F32),
            pltpu.VMEM((blocks, LANES), F32),
            pltpu.VMEM((peers, blocks, LANES), F32),
            pltpu.VMEM((everyone, PER, width), F32),
            pltpu.VMEM((PER, LANES), F32),
            pltpu.VMEM((peers, PER, LANES), F32),
            dma((7,)),
            dma((rows // (2 * LF),)),
            dma((blocks,)),
            dma((blocks,)),
            dma((fsdp_size,)),
            dma((fsdp_size,)),
            dma((peers,)),
            dma((peers,)),
            dma((everyone,)),
            dma((everyone,)),
            dma((peers,)),
            dma((peers,)),
        ],
        compiler_params=pltpu.CompilerParams(
            collective_id=0, has_side_effects=True, vmem_limit_bytes=VMEM_GRANT),
    )(*(pltpu.with_memory_space_constraint(a, pltpu.HBM) for a in (
        conv_input, gate, out_grad, filters.T, skip_bias.reshape(blocks, LANES))))
    if fused:
        input_grad, filter_part, bias_part = write_out(input_grad, filter_part, bias_part)
        return input_grad, filter_part.T, bias_part.reshape(chans)
    spread = lax.all_to_all(
        filter_part.reshape(groups, LF), "fsdp", split_axis=1, concat_axis=0, tiled=True)
    filter_grad, bias_grad = lax.psum((spread, bias_part.reshape(chans)), "seq")
    return input_grad, filter_grad, bias_grad


def solution(mesh):
    placed = (P("seq", "fsdp"), P("seq", "fsdp"), P("seq", "fsdp"), P(None, "fsdp"), P("fsdp"))
    return jax.shard_map(
        functools.partial(on_device, mesh.shape["seq"], mesh.shape["fsdp"]),
        mesh=mesh,
        in_specs=placed,
        out_specs=(P("seq", "fsdp"), P(None, "fsdp"), P("fsdp")),
        check_vma=False,
    )
```

```python
import functools

import jax
import jax.numpy as jnp
from jax import lax
from jax.experimental import pallas as pl
from jax.experimental.pallas import tpu as pltpu
from jax.sharding import PartitionSpec as P

GS = 16
VMEM_GRANT = 105 << 19
LF = 128
LANES = 128
PER = LANES // GS
LAYER = 2
MESH = pl.DeviceIdType.MESH
F32 = jnp.float32
BF16 = jnp.bfloat16


def kernel(
    seq_size, fsdp_size, fused,
    x_hbm, gate_hbm, og_hbm, filt_hbm, skip_hbm,
    ig_hbm, fg_ref, bias_ref,
    skip_ref, x_v, gate_v, og_v, sg_v, out_v, toep_v, taps_r, taps_v, part_v, bias_v,
    pack_v, send_v, recv_v,
    load_sem, out_sem, halo_send, halo_recv, tap_send, tap_recv, late_sem, term_send, term_recv,
):
    rows, chans = x_v.shape
    blocks = chans // LANES
    pairs = rows // (2 * LF)
    groups = chans // GS
    me_s = lax.axis_index("seq")
    me_f = lax.axis_index("fsdp")

    width = LF // fsdp_size
    sharing = LANES // groups

    def tap_lanes(owner):
        return pl.ds(pl.multiple_of(lax.div(owner, sharing) * LANES, LANES), LANES)

    def tap_rows(source):
        return pl.ds(pl.multiple_of(source * width, 8), width)

    rim = pl.ds(0, LF)
    rest = pl.ds(LF, rows - LF)
    loads = [
        pltpu.make_async_copy(og_hbm.at[rim], og_v.at[rim], load_sem.at[0]),
        pltpu.make_async_copy(gate_hbm.at[rim], gate_v.at[rim], load_sem.at[1]),
        pltpu.make_async_copy(og_hbm.at[rest], og_v.at[rest], load_sem.at[2]),
        pltpu.make_async_copy(gate_hbm.at[rest], gate_v.at[rest], load_sem.at[3]),
        pltpu.make_async_copy(x_hbm, x_v, load_sem.at[4]),
        pltpu.make_async_copy(
            filt_hbm.at[:, tap_lanes(me_f)], taps_r.at[tap_rows(me_f)], load_sem.at[5]),
        pltpu.make_async_copy(skip_hbm, skip_ref, load_sem.at[6]),
    ]
    for load in loads:
        load.start()

    barrier = pltpu.get_barrier_semaphore()
    layer_first = lax.div(me_s, LAYER) * LAYER if fused else 0
    layer_end = layer_first + LAYER if fused else 0
    per_layer = LAYER * fsdp_size

    def greet(semaphore, first, end):
        def step(other, c):
            o_s, o_f = lax.div(other, fsdp_size), lax.rem(other, fsdp_size)
            pl.semaphore_signal(
                semaphore, inc=1, device_id=(o_s, o_f), device_id_type=MESH)
            return c

        lax.fori_loop(first, end, step, 0)

    if fused:
        me = me_s * fsdp_size + me_f
        total = seq_size * fsdp_size
        greet(barrier, layer_first * fsdp_size, me)
        greet(barrier, me + 1, total)
    else:
        for d in range(1, fsdp_size):
            pl.semaphore_signal(
                barrier, inc=1, device_id=(me_s, lax.rem(me_f + d, fsdp_size)),
                device_id_type=MESH)

        @pl.when(me_s > 0)
        def _():
            pl.semaphore_signal(
                barrier, inc=1, device_id=(me_s - 1, me_f), device_id_type=MESH)

        @pl.when(me_s < seq_size - 1)
        def _():
            pl.semaphore_signal(
                barrier, inc=1, device_id=(me_s + 1, me_f), device_id_type=MESH)

    loads[0].wait()
    loads[1].wait()
    sg_v[rim, :] = (og_v[rim, :].astype(F32) * gate_v[rim, :].astype(F32)).astype(BF16)

    if fused:
        pl.semaphore_wait(barrier, layer_first * fsdp_size + per_layer - 1)
    else:
        pl.semaphore_wait(barrier, fsdp_size - 1)

        @pl.when(me_s > 0)
        def _():
            pl.semaphore_wait(barrier, 1)

        @pl.when(me_s < seq_size - 1)
        def _():
            pl.semaphore_wait(barrier, 1)

    def lanes_of(b):
        return pl.ds(pl.multiple_of(b * LANES, LANES), LANES)

    def halo_copy(target, b):
        return pltpu.make_async_remote_copy(
            src_ref=sg_v.at[rim, lanes_of(b)], dst_ref=sg_v.at[pl.ds(rows, LF), lanes_of(b)],
            send_sem=halo_send.at[b], recv_sem=halo_recv.at[b],
            device_id=(target, me_f), device_id_type=MESH)

    def each_block(do):
        def step(b, c):
            do(b)
            return c
        lax.fori_loop(0, blocks, step, 0)

    @pl.when(me_s > 0)
    def _():
        each_block(lambda b: halo_copy(me_s - 1, b).start())

    def tap_copy(d):
        other = lax.rem(me_f + d, fsdp_size)
        return pltpu.make_async_remote_copy(
            src_ref=filt_hbm.at[:, tap_lanes(other)],
            dst_ref=taps_r.at[tap_rows(me_f)],
            send_sem=tap_send.at[other], recv_sem=tap_recv.at[me_f],
            device_id=(me_s, other), device_id_type=MESH)

    def tap_arrival(d):
        other = lax.rem(me_f + d, fsdp_size)
        return pltpu.make_async_remote_copy(
            src_ref=filt_hbm.at[:, tap_lanes(other)],
            dst_ref=taps_r.at[tap_rows(other)],
            send_sem=tap_send.at[other], recv_sem=tap_recv.at[other],
            device_id=(me_s, other), device_id_type=MESH)

    for d in range(1, fsdp_size):
        tap_copy(d).start()

    if fused:
        greet(late_sem, 0, layer_first * fsdp_size)

    @pl.when(me_s == seq_size - 1)
    def _():
        sg_v[pl.ds(rows, LF), :] = jnp.zeros((LF, chans), BF16)

    for load in loads[2:5]:
        load.wait()

    def scale(b, c):
        lanes = lanes_of(b)
        new = (og_v[rest, lanes].astype(F32) * gate_v[rest, lanes].astype(F32)).astype(BF16)
        sg_v[rest, lanes] = new
        terms = jnp.sum(new.astype(F32) * x_v[rest, lanes].astype(F32), axis=0, keepdims=True)
        terms = terms + jnp.sum(
            sg_v[rim, lanes].astype(F32) * x_v[rim, lanes].astype(F32), axis=0, keepdims=True)
        bias_v[pl.ds(b, 1), :] = terms
        return c

    lax.fori_loop(0, blocks, scale, 0, unroll=2)

    row_at = lax.broadcasted_iota(jnp.int32, (LF, LANES), 0)
    lane_at = lax.broadcasted_iota(jnp.int32, (LF, LANES), 1)
    above = lane_at >= row_at

    def windows(p, lanes):
        at = 2 * LF * p
        return jnp.concatenate(
            [sg_v[at:at + 2 * LF, lanes], sg_v[at + LF:at + 3 * LF, lanes]], axis=1)

    def split_groups(both):
        lane = lax.broadcasted_iota(jnp.int32, both.shape, 1)
        owner = lax.rem(lax.div(lane, GS), PER)
        return jnp.concatenate(
            [both * (owner == g).astype(F32).astype(BF16) for g in range(PER)], axis=0)

    def products(left, right):
        return lax.dot_general(
            split_groups(left), right, (((1,), (1,)), ((), ())), preferred_element_type=F32)

    def fold(wrapped):
        total = wrapped[:8]
        for k in range(1, LF // 8):
            total = total + pltpu.roll(wrapped[8 * k:8 * k + 8], LANES - 8 * k, 1)
        return total

    sub = lax.broadcasted_iota(jnp.int32, (8, LANES), 0)

    def correlate(b, c):
        lanes = lanes_of(b)

        @pl.when(me_s < seq_size - 1)
        def _():
            halo_copy(me_s + 1, b).wait_recv()

        left = jnp.concatenate([x_v[at:at + LF, lanes] for at in range(0, rows, LF)], axis=1)
        right = jnp.concatenate(
            [sg_v[at:at + 2 * LF, lanes] for at in range(0, rows, LF)], axis=1)
        prod = products(left, right)
        out = jnp.zeros((8, LANES), F32)
        for g in range(PER):
            one = prod[g * LF:(g + 1) * LF]
            whole = fold(jnp.where(above, one[:, :LANES], one[:, LANES:]))
            for bit in range(3):
                whole = jnp.where(
                    lax.rem(lax.div(sub, 1 << bit), 2) == 1,
                    pltpu.roll(whole, LANES - (1 << bit), 1), whole)
            out = jnp.where(sub == g, jnp.sum(whole, axis=0, keepdims=True), out)
        part_v[pl.ds(pl.multiple_of(b * PER, PER), PER), :] = out
        return c

    def build(b, c):
        first = lax.rem(me_f, sharing) * groups + b * PER
        taps = taps_v[pl.ds(pl.multiple_of(first, PER), PER), :]
        for g in range(PER):
            band = pltpu.roll(
                jnp.broadcast_to(taps[g:g + 1], (LF, LANES)), 0, 1, stride=1, stride_axis=0)
            zero = jnp.zeros_like(band)
            toep_v[b, g * LF:(g + 1) * LF, :LANES] = jnp.where(above, band, zero).astype(BF16)
            toep_v[b, g * LF:(g + 1) * LF, LANES:] = jnp.where(above, zero, band).astype(BF16)
        return c

    def conv(b, c, p):
        lanes = lanes_of(b)
        at = 2 * LF * p
        prod = jnp.dot(toep_v[b], windows(p, lanes), preferred_element_type=F32)
        owner = lax.div(lax.broadcasted_iota(jnp.int32, (LF, 2 * LANES), 1), GS)
        owner = lax.rem(owner, PER)
        out = prod[:LF]
        for g in range(1, PER):
            out = jnp.where(owner == g, prod[g * LF:(g + 1) * LF], out)
        skip = skip_ref[pl.ds(b, 1), :]
        for half in range(2):
            here = slice(at + half * LF, at + (half + 1) * LF)
            direct = skip * sg_v[here, lanes].astype(F32)
            out_v[here, lanes] = (
                out[:, half * LANES:(half + 1) * LANES] + direct).astype(BF16)
        return c

    lax.fori_loop(0, blocks, correlate, 0, unroll=2)

    if fused:
        half_taps = width // 2
        pack_v[:groups, :] = part_v[...]
        pack_v[groups:, :] = pltpu.roll(part_v[...], LANES - half_taps, 1)
        turned = pack_v[...].T.astype(BF16)
        high = bias_v[...].astype(BF16)
        low = (bias_v[...] - high.astype(F32)).astype(BF16)
        for f in range(fsdp_size):
            send_v[f, :half_taps, :] = turned[f * width:f * width + half_taps]
            send_v[f, half_taps:, :] = jnp.concatenate([high, low], axis=0)
        recv_v[me] = send_v[me_f]

        @pl.when(layer_end < seq_size)
        def _():
            pl.semaphore_wait(late_sem, (seq_size - layer_end) * fsdp_size)

        def term_copy(d_s, d_f, arrival):
            o_s = lax.rem(me_s + d_s, seq_size)
            o_f = lax.rem(me_f + d_f, fsdp_size)
            other = o_s * fsdp_size + o_f
            at = other if arrival else me
            span = pl.ds(0, 2 * half_taps if d_f == 0 else half_taps)
            return pltpu.make_async_remote_copy(
                src_ref=send_v.at[o_f, span], dst_ref=recv_v.at[at, span],
                send_sem=term_send.at[other], recv_sem=term_recv.at[at],
                device_id=(o_s, o_f), device_id_type=MESH)

        def each_other(do):
            def step(i, c):
                d_s = lax.rem(i + seq_size // 2, seq_size)
                for d_f in range(fsdp_size):
                    do(d_s, d_f)
                return c

            lax.fori_loop(0, seq_size // 2, step, 0)
            lax.fori_loop(seq_size // 2 + 1, seq_size, step, 0)
            for d_f in range(1, fsdp_size):
                do(0, d_f)

        each_other(lambda d_s, d_f: term_copy(d_s, d_f, False).start())

    loads[5].wait()
    loads[6].wait()
    for d in range(1, fsdp_size):
        tap_arrival(d).wait_recv()
    taps_v[...] = taps_r[...].T
    lax.fori_loop(0, blocks, build, 0, unroll=2)

    def out_copy(p):
        span = pl.ds(2 * LF * p, 2 * LF)
        return pltpu.make_async_copy(out_v.at[span], ig_hbm.at[span], out_sem.at[p])

    for p in range(pairs):
        lax.fori_loop(0, blocks, functools.partial(conv, p=p), 0, unroll=2)
        out_copy(p).start()

    for d in range(1, fsdp_size):
        tap_copy(d).wait_send()

    @pl.when(me_s > 0)
    def _():
        each_block(lambda b: halo_copy(me_s - 1, b).wait_send())

    if fused:
        each_other(lambda d_s, d_f: term_copy(d_s, d_f, False).wait_send())
        each_other(lambda d_s, d_f: term_copy(d_s, d_f, True).wait_recv())
        lane = lax.broadcasted_iota(jnp.int32, (half_taps, LANES), 1)
        sums = []
        for f in range(fsdp_size):
            piece = recv_v[f, :half_taps].astype(F32)
            for k in range(1, seq_size):
                piece = piece + recv_v[k * fsdp_size + f, :half_taps].astype(F32)
            sums.append(piece)
        for f in range(0, fsdp_size, 2):
            pair = pl.ds(f * groups, 2 * groups)
            fg_ref[:half_taps, pair] = jnp.where(
                lane < groups, sums[f], pltpu.roll(sums[f + 1], groups, 1))
            fg_ref[half_taps:, pair] = jnp.where(
                lane < groups, pltpu.roll(sums[f], groups, 1), sums[f + 1])
        both = recv_v[me_f, half_taps:].astype(F32)
        for k in range(1, seq_size):
            both = both + recv_v[k * fsdp_size + me_f, half_taps:].astype(F32)
        bias_ref[...] = both[:blocks] + both[blocks:]
    else:
        fg_ref[...] = part_v[...]
        bias_ref[...] = bias_v[...]
    for p in range(pairs):
        out_copy(p).wait()


def writer(*refs):
    count = len(refs) // 2
    sources, targets, sems = refs[:count], refs[count:2 * count], refs[2 * count]
    copies = [
        pltpu.make_async_copy(a, b, sems.at[i]) for i, (a, b) in enumerate(zip(sources, targets))]
    for copy in copies:
        copy.start()
    for copy in copies:
        copy.wait()


def write_out(*arrays):
    return pl.pallas_call(
        writer,
        out_shape=tuple(pltpu.HBM(a.shape, a.dtype) for a in arrays),
        in_specs=[pl.BlockSpec(memory_space=pltpu.VMEM)] * len(arrays),
        out_specs=(pl.BlockSpec(memory_space=pltpu.HBM),) * len(arrays),
        scratch_shapes=[pltpu.SemaphoreType.DMA((len(arrays),))],
    )(*(pltpu.with_memory_space_constraint(a, pltpu.VMEM) for a in arrays))


def on_device(seq_size, fsdp_size, conv_input, gate, out_grad, filters, skip_bias):
    rows, chans = conv_input.shape
    blocks = chans // LANES
    groups = chans // GS
    width = LF // fsdp_size
    fused = (
        seq_size % LAYER == 0 and seq_size <= 8 and fsdp_size % 2 == 0
        and 2 * groups == LANES and 2 * blocks == width // 2)
    everyone = seq_size * fsdp_size if fused else 1
    fg_shape = (width, fsdp_size * groups) if fused else (groups, LF)
    term_rows = width if fused else 32
    hbm_spec = pl.BlockSpec(memory_space=pltpu.HBM)
    vmem_spec = pl.BlockSpec(memory_space=pltpu.VMEM)
    dma = pltpu.SemaphoreType.DMA
    input_grad, filter_part, bias_part = pl.pallas_call(
        functools.partial(kernel, seq_size, fsdp_size, fused),
        out_shape=(
            jax.ShapeDtypeStruct((rows, chans), BF16),
            jax.ShapeDtypeStruct(fg_shape, F32),
            jax.ShapeDtypeStruct((blocks, LANES), F32),
        ),
        in_specs=[hbm_spec] * 5,
        out_specs=(hbm_spec, vmem_spec, vmem_spec),
        scratch_shapes=[
            pltpu.VMEM((blocks, LANES), F32),
            pltpu.VMEM((rows, chans), BF16),
            pltpu.VMEM((rows, chans), BF16),
            pltpu.VMEM((rows, chans), BF16),
            pltpu.VMEM((rows + LF, chans), BF16),
            pltpu.VMEM((rows, chans), BF16),
            pltpu.VMEM((blocks, PER * LF, 2 * LANES), BF16),
            pltpu.VMEM((LF, LANES), F32),
            pltpu.VMEM((LANES, LF), F32),
            pltpu.VMEM((groups, LANES), F32),
            pltpu.VMEM((blocks, LANES), F32),
            pltpu.VMEM((2 * groups, LANES), F32),
            pltpu.VMEM((fsdp_size, term_rows, LANES), BF16),
            pltpu.VMEM((everyone, term_rows, LANES), BF16),
            dma((7,)),
            dma((rows // (2 * LF),)),
            dma((blocks,)),
            dma((blocks,)),
            dma((fsdp_size,)),
            dma((fsdp_size,)),
            pltpu.SemaphoreType.REGULAR,
            dma((everyone,)),
            dma((everyone,)),
        ],
        compiler_params=pltpu.CompilerParams(
            collective_id=0, has_side_effects=True, vmem_limit_bytes=VMEM_GRANT),
    )(*(pltpu.with_memory_space_constraint(a, pltpu.HBM) for a in (
        conv_input, gate, out_grad, filters.T, skip_bias.reshape(blocks, LANES))))
    if fused:
        input_grad, filter_part, bias_part = write_out(input_grad, filter_part, bias_part)
        return input_grad, filter_part.T, bias_part.reshape(chans)
    spread = lax.all_to_all(
        filter_part, "fsdp", split_axis=1, concat_axis=0, tiled=True)
    filter_grad, bias_grad = lax.psum((spread, bias_part.reshape(chans)), "seq")
    return input_grad, filter_grad, bias_grad


def solution(mesh):
    placed = (P("seq", "fsdp"), P("seq", "fsdp"), P("seq", "fsdp"), P(None, "fsdp"), P("fsdp"))
    return jax.shard_map(
        functools.partial(on_device, mesh.shape["seq"], mesh.shape["fsdp"]),
        mesh=mesh,
        in_specs=placed,
        out_specs=(P("seq", "fsdp"), P(None, "fsdp"), P("fsdp")),
        check_vma=False,
    )
```

```python
import functools

import jax
import jax.numpy as jnp
from jax import lax
from jax.experimental import pallas as pl
from jax.experimental.pallas import tpu as pltpu
from jax.sharding import PartitionSpec as P

GS = 16
VMEM_GRANT = 105 << 19
LF = 128
LANES = 128
PER = LANES // GS
LAYER = 2
MESH = pl.DeviceIdType.MESH
F32 = jnp.float32
BF16 = jnp.bfloat16


def kernel(
    seq_size, fsdp_size, fused,
    x_hbm, gate_hbm, og_hbm, filt_hbm, skip_hbm,
    ig_hbm, fg_ref, bias_ref,
    skip_ref, x_v, gate_v, og_v, sg_v, out_v, toep_v, taps_r, taps_v, part_v, bias_v,
    pack_v, send_v, recv_v,
    load_sem, out_sem, halo_send, halo_recv, tap_send, tap_recv, late_sem, term_send, term_recv,
):
    rows, chans = x_v.shape
    blocks = chans // LANES
    pairs = rows // (2 * LF)
    groups = chans // GS
    me_s = lax.axis_index("seq")
    me_f = lax.axis_index("fsdp")

    width = LF // fsdp_size
    sharing = LANES // groups

    def tap_lanes(owner):
        return pl.ds(pl.multiple_of(lax.div(owner, sharing) * LANES, LANES), LANES)

    def tap_rows(source):
        return pl.ds(pl.multiple_of(source * width, 8), width)

    rim = pl.ds(0, LF)
    rest = pl.ds(LF, rows - LF)
    loads = [
        pltpu.make_async_copy(og_hbm.at[rim], og_v.at[rim], load_sem.at[0]),
        pltpu.make_async_copy(gate_hbm.at[rim], gate_v.at[rim], load_sem.at[1]),
        pltpu.make_async_copy(og_hbm.at[rest], og_v.at[rest], load_sem.at[2]),
        pltpu.make_async_copy(gate_hbm.at[rest], gate_v.at[rest], load_sem.at[3]),
        pltpu.make_async_copy(x_hbm, x_v, load_sem.at[4]),
        pltpu.make_async_copy(
            filt_hbm.at[:, tap_lanes(me_f)], taps_r.at[tap_rows(me_f)], load_sem.at[5]),
        pltpu.make_async_copy(skip_hbm, skip_ref, load_sem.at[6]),
    ]
    for load in loads:
        load.start()

    barrier = pltpu.get_barrier_semaphore()
    layer_first = lax.div(me_s, LAYER) * LAYER if fused else 0
    layer_end = layer_first + LAYER if fused else 0
    per_layer = LAYER * fsdp_size

    def greet(semaphore, first, end):
        def step(other, c):
            o_s, o_f = lax.div(other, fsdp_size), lax.rem(other, fsdp_size)
            pl.semaphore_signal(
                semaphore, inc=1, device_id=(o_s, o_f), device_id_type=MESH)
            return c

        lax.fori_loop(first, end, step, 0)

    if fused:
        me = me_s * fsdp_size + me_f
        total = seq_size * fsdp_size
        greet(barrier, layer_first * fsdp_size, me)
        greet(barrier, me + 1, total)
    else:
        for d in range(1, fsdp_size):
            pl.semaphore_signal(
                barrier, inc=1, device_id=(me_s, lax.rem(me_f + d, fsdp_size)),
                device_id_type=MESH)

        @pl.when(me_s > 0)
        def _():
            pl.semaphore_signal(
                barrier, inc=1, device_id=(me_s - 1, me_f), device_id_type=MESH)

        @pl.when(me_s < seq_size - 1)
        def _():
            pl.semaphore_signal(
                barrier, inc=1, device_id=(me_s + 1, me_f), device_id_type=MESH)

    loads[0].wait()
    loads[1].wait()
    sg_v[rim, :] = (og_v[rim, :].astype(F32) * gate_v[rim, :].astype(F32)).astype(BF16)

    if fused:
        pl.semaphore_wait(barrier, layer_first * fsdp_size + per_layer - 1)
    else:
        pl.semaphore_wait(barrier, fsdp_size - 1)

        @pl.when(me_s > 0)
        def _():
            pl.semaphore_wait(barrier, 1)

        @pl.when(me_s < seq_size - 1)
        def _():
            pl.semaphore_wait(barrier, 1)

    def lanes_of(b):
        return pl.ds(pl.multiple_of(b * LANES, LANES), LANES)

    def halo_copy(target, b):
        return pltpu.make_async_remote_copy(
            src_ref=sg_v.at[rim, lanes_of(b)], dst_ref=sg_v.at[pl.ds(rows, LF), lanes_of(b)],
            send_sem=halo_send.at[b], recv_sem=halo_recv.at[b],
            device_id=(target, me_f), device_id_type=MESH)

    def each_block(do):
        def step(b, c):
            do(b)
            return c
        lax.fori_loop(0, blocks, step, 0)

    @pl.when(me_s > 0)
    def _():
        each_block(lambda b: halo_copy(me_s - 1, b).start())

    def tap_copy(d):
        other = lax.rem(me_f + d, fsdp_size)
        return pltpu.make_async_remote_copy(
            src_ref=filt_hbm.at[:, tap_lanes(other)],
            dst_ref=taps_r.at[tap_rows(me_f)],
            send_sem=tap_send.at[other], recv_sem=tap_recv.at[me_f],
            device_id=(me_s, other), device_id_type=MESH)

    def tap_arrival(d):
        other = lax.rem(me_f + d, fsdp_size)
        return pltpu.make_async_remote_copy(
            src_ref=filt_hbm.at[:, tap_lanes(other)],
            dst_ref=taps_r.at[tap_rows(other)],
            send_sem=tap_send.at[other], recv_sem=tap_recv.at[other],
            device_id=(me_s, other), device_id_type=MESH)

    for d in range(1, fsdp_size):
        tap_copy(d).start()

    if fused:
        greet(late_sem, 0, layer_first * fsdp_size)

    @pl.when(me_s == seq_size - 1)
    def _():
        sg_v[pl.ds(rows, LF), :] = jnp.zeros((LF, chans), BF16)

    for load in loads[2:5]:
        load.wait()

    def scale(b, c):
        lanes = lanes_of(b)
        new = (og_v[rest, lanes].astype(F32) * gate_v[rest, lanes].astype(F32)).astype(BF16)
        sg_v[rest, lanes] = new
        terms = jnp.sum(new.astype(F32) * x_v[rest, lanes].astype(F32), axis=0, keepdims=True)
        terms = terms + jnp.sum(
            sg_v[rim, lanes].astype(F32) * x_v[rim, lanes].astype(F32), axis=0, keepdims=True)
        bias_v[pl.ds(b, 1), :] = terms
        return c

    lax.fori_loop(0, blocks, scale, 0, unroll=2)

    row_at = lax.broadcasted_iota(jnp.int32, (LF, LANES), 0)
    lane_at = lax.broadcasted_iota(jnp.int32, (LF, LANES), 1)
    above = lane_at >= row_at

    def windows(p, lanes):
        at = 2 * LF * p
        return jnp.concatenate(
            [sg_v[at:at + 2 * LF, lanes], sg_v[at + LF:at + 3 * LF, lanes]], axis=1)

    def split_groups(both):
        lane = lax.broadcasted_iota(jnp.int32, both.shape, 1)
        owner = lax.rem(lax.div(lane, GS), PER)
        return jnp.concatenate(
            [both * (owner == g).astype(F32).astype(BF16) for g in range(PER)], axis=0)

    def products(left, right):
        return lax.dot_general(
            split_groups(left), right, (((1,), (1,)), ((), ())), preferred_element_type=F32)

    def fold(wrapped):
        parts = [wrapped[:8]] + [
            pltpu.roll(wrapped[8 * k:8 * k + 8], LANES - 8 * k, 1) for k in range(1, LF // 8)]
        while len(parts) > 1:
            parts = [one + two for one, two in zip(parts[::2], parts[1::2])]
        return parts[0]

    sub = lax.broadcasted_iota(jnp.int32, (8, LANES), 0)

    def diagonals(wholes):
        for bit in (2, 1, 0):
            step = 1 << bit
            odd = lax.rem(lax.div(sub, step), 2) == 1
            wholes = [
                jnp.where(odd, pltpu.roll(wholes[i + step], step, 0), wholes[i])
                + pltpu.roll(
                    jnp.where(odd, wholes[i + step], pltpu.roll(wholes[i], 8 - step, 0)),
                    LANES - step, 1)
                for i in range(step)]
        return wholes[0]

    def correlate(b):
        lanes = lanes_of(b)
        left = jnp.concatenate([x_v[at:at + LF, lanes] for at in range(0, rows, LF)], axis=1)
        right = jnp.concatenate(
            [sg_v[at:at + 2 * LF, lanes] for at in range(0, rows, LF)], axis=1)
        prod = products(left, right)
        wholes = []
        for g in range(PER):
            one = prod[g * LF:(g + 1) * LF]
            wholes.append(fold(jnp.where(above, one[:, :LANES], one[:, LANES:])))
        part_v[pl.ds(pl.multiple_of(b * PER, PER), PER), :] = diagonals(wholes)

    def correlate_two(i, c):
        @pl.when(me_s < seq_size - 1)
        def _():
            halo_copy(me_s + 1, 2 * i).wait_recv()
            halo_copy(me_s + 1, 2 * i + 1).wait_recv()

        correlate(2 * i)
        correlate(2 * i + 1)
        return c

    def build(b, c):
        first = lax.rem(me_f, sharing) * groups + b * PER
        taps = taps_v[pl.ds(pl.multiple_of(first, PER), PER), :]
        for g in range(PER):
            band = pltpu.roll(
                jnp.broadcast_to(taps[g:g + 1], (LF, LANES)), 0, 1, stride=1, stride_axis=0)
            zero = jnp.zeros_like(band)
            toep_v[b, g * LF:(g + 1) * LF, :LANES] = jnp.where(above, band, zero).astype(BF16)
            toep_v[b, g * LF:(g + 1) * LF, LANES:] = jnp.where(above, zero, band).astype(BF16)
        return c

    def conv(b, c, p):
        lanes = lanes_of(b)
        at = 2 * LF * p
        prod = jnp.dot(toep_v[b], windows(p, lanes), preferred_element_type=F32)
        owner = lax.div(lax.broadcasted_iota(jnp.int32, (LF, 2 * LANES), 1), GS)
        owner = lax.rem(owner, PER)
        out = prod[:LF]
        for g in range(1, PER):
            out = jnp.where(owner == g, prod[g * LF:(g + 1) * LF], out)
        skip = skip_ref[pl.ds(b, 1), :]
        for half in range(2):
            here = slice(at + half * LF, at + (half + 1) * LF)
            direct = skip * sg_v[here, lanes].astype(F32)
            out_v[here, lanes] = (
                out[:, half * LANES:(half + 1) * LANES] + direct).astype(BF16)
        return c

    lax.fori_loop(0, blocks // 2, correlate_two, 0)

    if fused:
        half_taps = width // 2
        pack_v[:groups, :] = part_v[...]
        pack_v[groups:, :] = pltpu.roll(part_v[...], LANES - half_taps, 1)
        turned = pack_v[...].T.astype(BF16)
        high = bias_v[...].astype(BF16)
        low = (bias_v[...] - high.astype(F32)).astype(BF16)
        for f in range(fsdp_size):
            send_v[f, :half_taps, :] = turned[f * width:f * width + half_taps]
            send_v[f, half_taps:, :] = jnp.concatenate([high, low], axis=0)
        recv_v[me] = send_v[me_f]

        @pl.when(layer_end < seq_size)
        def _():
            pl.semaphore_wait(late_sem, (seq_size - layer_end) * fsdp_size)

        def term_copy(o_s, d_f, arrival):
            o_f = lax.rem(me_f + d_f, fsdp_size)
            other = o_s * fsdp_size + o_f
            at = other if arrival else me
            span = pl.ds(0, 2 * half_taps if d_f == 0 else half_taps)
            return pltpu.make_async_remote_copy(
                src_ref=send_v.at[o_f, span], dst_ref=recv_v.at[at, span],
                send_sem=term_send.at[other], recv_sem=term_recv.at[at],
                device_id=(o_s, o_f), device_id_type=MESH)

        upper = lax.div(me_s, seq_size // 2)

        def each_other(do):
            def step(i, c):
                mine = upper * me_s + (1 - upper) * (seq_size - 1 - me_s)
                at = i + lax.div(i + seq_size - mine, seq_size)
                o_s = upper * at + (1 - upper) * (seq_size - 1 - at)
                for d_f in range(fsdp_size):
                    do(o_s, d_f)
                return c

            lax.fori_loop(0, seq_size - 1, step, 0)
            for d_f in range(1, fsdp_size):
                do(me_s, d_f)

        each_other(lambda d_s, d_f: term_copy(d_s, d_f, False).start())

    loads[5].wait()
    loads[6].wait()
    for d in range(1, fsdp_size):
        tap_arrival(d).wait_recv()
    taps_v[...] = taps_r[...].T
    lax.fori_loop(0, blocks, build, 0, unroll=2)

    def out_copy(p):
        span = pl.ds(2 * LF * p, 2 * LF)
        return pltpu.make_async_copy(out_v.at[span], ig_hbm.at[span], out_sem.at[p])

    for p in range(pairs):
        lax.fori_loop(0, blocks, functools.partial(conv, p=p), 0, unroll=2)
        out_copy(p).start()

    for d in range(1, fsdp_size):
        tap_copy(d).wait_send()

    @pl.when(me_s > 0)
    def _():
        each_block(lambda b: halo_copy(me_s - 1, b).wait_send())

    if fused:
        each_other(lambda d_s, d_f: term_copy(d_s, d_f, False).wait_send())
        each_other(lambda d_s, d_f: term_copy(d_s, d_f, True).wait_recv())
        lane = lax.broadcasted_iota(jnp.int32, (half_taps, LANES), 1)
        sums = []
        for f in range(fsdp_size):
            piece = recv_v[f, :half_taps].astype(F32)
            for k in range(1, seq_size):
                piece = piece + recv_v[k * fsdp_size + f, :half_taps].astype(F32)
            sums.append(piece)
        for f in range(0, fsdp_size, 2):
            pair = pl.ds(f * groups, 2 * groups)
            fg_ref[:half_taps, pair] = jnp.where(
                lane < groups, sums[f], pltpu.roll(sums[f + 1], groups, 1))
            fg_ref[half_taps:, pair] = jnp.where(
                lane < groups, pltpu.roll(sums[f], groups, 1), sums[f + 1])
        both = recv_v[me_f, half_taps:].astype(F32)
        for k in range(1, seq_size):
            both = both + recv_v[k * fsdp_size + me_f, half_taps:].astype(F32)
        bias_ref[...] = both[:blocks] + both[blocks:]
    else:
        fg_ref[...] = part_v[...]
        bias_ref[...] = bias_v[...]
    for p in range(pairs):
        out_copy(p).wait()


def writer(*refs):
    count = len(refs) // 2
    sources, targets, sems = refs[:count], refs[count:2 * count], refs[2 * count]
    copies = [
        pltpu.make_async_copy(a, b, sems.at[i]) for i, (a, b) in enumerate(zip(sources, targets))]
    for copy in copies:
        copy.start()
    for copy in copies:
        copy.wait()


def write_out(*arrays):
    return pl.pallas_call(
        writer,
        out_shape=tuple(pltpu.HBM(a.shape, a.dtype) for a in arrays),
        in_specs=[pl.BlockSpec(memory_space=pltpu.VMEM)] * len(arrays),
        out_specs=(pl.BlockSpec(memory_space=pltpu.HBM),) * len(arrays),
        scratch_shapes=[pltpu.SemaphoreType.DMA((len(arrays),))],
    )(*(pltpu.with_memory_space_constraint(a, pltpu.VMEM) for a in arrays))


def on_device(seq_size, fsdp_size, conv_input, gate, out_grad, filters, skip_bias):
    rows, chans = conv_input.shape
    blocks = chans // LANES
    groups = chans // GS
    width = LF // fsdp_size
    fused = (
        seq_size % LAYER == 0 and seq_size <= 8 and fsdp_size % 2 == 0
        and 2 * groups == LANES and 2 * blocks == width // 2)
    everyone = seq_size * fsdp_size if fused else 1
    fg_shape = (width, fsdp_size * groups) if fused else (groups, LF)
    term_rows = width if fused else 32
    hbm_spec = pl.BlockSpec(memory_space=pltpu.HBM)
    vmem_spec = pl.BlockSpec(memory_space=pltpu.VMEM)
    dma = pltpu.SemaphoreType.DMA
    input_grad, filter_part, bias_part = pl.pallas_call(
        functools.partial(kernel, seq_size, fsdp_size, fused),
        out_shape=(
            jax.ShapeDtypeStruct((rows, chans), BF16),
            jax.ShapeDtypeStruct(fg_shape, F32),
            jax.ShapeDtypeStruct((blocks, LANES), F32),
        ),
        in_specs=[hbm_spec] * 5,
        out_specs=(hbm_spec, vmem_spec, vmem_spec),
        scratch_shapes=[
            pltpu.VMEM((blocks, LANES), F32),
            pltpu.VMEM((rows, chans), BF16),
            pltpu.VMEM((rows, chans), BF16),
            pltpu.VMEM((rows, chans), BF16),
            pltpu.VMEM((rows + LF, chans), BF16),
            pltpu.VMEM((rows, chans), BF16),
            pltpu.VMEM((blocks, PER * LF, 2 * LANES), BF16),
            pltpu.VMEM((LF, LANES), F32),
            pltpu.VMEM((LANES, LF), F32),
            pltpu.VMEM((groups, LANES), F32),
            pltpu.VMEM((blocks, LANES), F32),
            pltpu.VMEM((2 * groups, LANES), F32),
            pltpu.VMEM((fsdp_size, term_rows, LANES), BF16),
            pltpu.VMEM((everyone, term_rows, LANES), BF16),
            dma((7,)),
            dma((rows // (2 * LF),)),
            dma((blocks,)),
            dma((blocks,)),
            dma((fsdp_size,)),
            dma((fsdp_size,)),
            pltpu.SemaphoreType.REGULAR,
            dma((everyone,)),
            dma((everyone,)),
        ],
        compiler_params=pltpu.CompilerParams(
            collective_id=0, has_side_effects=True, vmem_limit_bytes=VMEM_GRANT),
    )(*(pltpu.with_memory_space_constraint(a, pltpu.HBM) for a in (
        conv_input, gate, out_grad, filters.T, skip_bias.reshape(blocks, LANES))))
    if fused:
        input_grad, filter_part, bias_part = write_out(input_grad, filter_part, bias_part)
        return input_grad, filter_part.T, bias_part.reshape(chans)
    spread = lax.all_to_all(
        filter_part, "fsdp", split_axis=1, concat_axis=0, tiled=True)
    filter_grad, bias_grad = lax.psum((spread, bias_part.reshape(chans)), "seq")
    return input_grad, filter_grad, bias_grad


def solution(mesh):
    placed = (P("seq", "fsdp"), P("seq", "fsdp"), P("seq", "fsdp"), P(None, "fsdp"), P("fsdp"))
    return jax.shard_map(
        functools.partial(on_device, mesh.shape["seq"], mesh.shape["fsdp"]),
        mesh=mesh,
        in_specs=placed,
        out_specs=(P("seq", "fsdp"), P(None, "fsdp"), P("fsdp")),
        check_vma=False,
    )
```

```python
import functools

import jax
import jax.numpy as jnp
from jax import lax
from jax.experimental import pallas as pl
from jax.experimental.pallas import tpu as pltpu
from jax.sharding import PartitionSpec as P

GS = 16
VMEM_GRANT = 105 << 19
LF = 128
LANES = 128
PER = LANES // GS
LAYER = 2
MESH = pl.DeviceIdType.MESH
F32 = jnp.float32
BF16 = jnp.bfloat16


def kernel(
    seq_size, fsdp_size, fused,
    x_hbm, gate_hbm, og_hbm, filt_hbm, skip_hbm,
    ig_hbm, fg_ref, bias_ref,
    skip_ref, x_v, gate_v, og_v, sg_v, out_v, toep_v, taps_r, taps_v, part_v, bias_v,
    pack_v, send_v, recv_v, sums_v,
    load_sem, out_sem, halo_send, halo_recv, tap_send, tap_recv, late_sem, term_send, term_recv,
):
    rows, chans = x_v.shape
    blocks = chans // LANES
    pairs = rows // (2 * LF)
    groups = chans // GS
    me_s = lax.axis_index("seq")
    me_f = lax.axis_index("fsdp")

    width = LF // fsdp_size
    sharing = LANES // groups

    def tap_lanes(owner):
        return pl.ds(pl.multiple_of(lax.div(owner, sharing) * LANES, LANES), LANES)

    def tap_rows(source):
        return pl.ds(pl.multiple_of(source * width, 8), width)

    rim = pl.ds(0, LF)
    rest = pl.ds(LF, rows - LF)
    loads = [
        pltpu.make_async_copy(og_hbm.at[rim], og_v.at[rim], load_sem.at[0]),
        pltpu.make_async_copy(gate_hbm.at[rim], gate_v.at[rim], load_sem.at[1]),
        pltpu.make_async_copy(og_hbm.at[rest], og_v.at[rest], load_sem.at[2]),
        pltpu.make_async_copy(gate_hbm.at[rest], gate_v.at[rest], load_sem.at[3]),
        pltpu.make_async_copy(x_hbm, x_v, load_sem.at[4]),
        pltpu.make_async_copy(
            filt_hbm.at[:, tap_lanes(me_f)], taps_r.at[tap_rows(me_f)], load_sem.at[5]),
        pltpu.make_async_copy(skip_hbm, skip_ref, load_sem.at[6]),
    ]
    barrier = pltpu.get_barrier_semaphore()
    layer_first = lax.div(me_s, LAYER) * LAYER if fused else 0
    layer_end = layer_first + LAYER if fused else 0
    per_layer = LAYER * fsdp_size

    def greet(semaphore, first, end):
        def step(other, c):
            o_s, o_f = lax.div(other, fsdp_size), lax.rem(other, fsdp_size)
            pl.semaphore_signal(
                semaphore, inc=1, device_id=(o_s, o_f), device_id_type=MESH)
            return c

        lax.fori_loop(first, end, step, 0)

    if fused:
        me = me_s * fsdp_size + me_f
        total = seq_size * fsdp_size
        greet(barrier, layer_first * fsdp_size, me)
        greet(barrier, me + 1, layer_end * fsdp_size)
    else:
        for d in range(1, fsdp_size):
            pl.semaphore_signal(
                barrier, inc=1, device_id=(me_s, lax.rem(me_f + d, fsdp_size)),
                device_id_type=MESH)

        @pl.when(me_s > 0)
        def _():
            pl.semaphore_signal(
                barrier, inc=1, device_id=(me_s - 1, me_f), device_id_type=MESH)

        @pl.when(me_s < seq_size - 1)
        def _():
            pl.semaphore_signal(
                barrier, inc=1, device_id=(me_s + 1, me_f), device_id_type=MESH)

    for load in loads:
        load.start()
    if fused:
        greet(barrier, layer_end * fsdp_size, total)
    loads[0].wait()
    loads[1].wait()
    sg_v[rim, :] = (og_v[rim, :].astype(F32) * gate_v[rim, :].astype(F32)).astype(BF16)

    if fused:
        pl.semaphore_wait(barrier, layer_first * fsdp_size + per_layer - 1)
    else:
        pl.semaphore_wait(barrier, fsdp_size - 1)

        @pl.when(me_s > 0)
        def _():
            pl.semaphore_wait(barrier, 1)

        @pl.when(me_s < seq_size - 1)
        def _():
            pl.semaphore_wait(barrier, 1)

    def lanes_of(b):
        return pl.ds(pl.multiple_of(b * LANES, LANES), LANES)

    def halo_copy(target, first, end):
        lanes = pl.ds(first * LANES, (end - first) * LANES)
        return pltpu.make_async_remote_copy(
            src_ref=sg_v.at[rim, lanes], dst_ref=sg_v.at[pl.ds(rows, LF), lanes],
            send_sem=halo_send, recv_sem=halo_recv.at[first // 2],
            device_id=(target, me_f), device_id_type=MESH)

    @pl.when(me_s > 0)
    def _():
        for b in range(0, blocks, 2):
            halo_copy(me_s - 1, b, b + 2).start()

    def tap_copy(d):
        other = lax.rem(me_f + d, fsdp_size)
        return pltpu.make_async_remote_copy(
            src_ref=filt_hbm.at[:, tap_lanes(other)],
            dst_ref=taps_r.at[tap_rows(me_f)],
            send_sem=tap_send.at[other], recv_sem=tap_recv.at[me_f],
            device_id=(me_s, other), device_id_type=MESH)

    def tap_arrival(d):
        other = lax.rem(me_f + d, fsdp_size)
        return pltpu.make_async_remote_copy(
            src_ref=filt_hbm.at[:, tap_lanes(other)],
            dst_ref=taps_r.at[tap_rows(other)],
            send_sem=tap_send.at[other], recv_sem=tap_recv.at[other],
            device_id=(me_s, other), device_id_type=MESH)

    for d in range(1, fsdp_size):
        tap_copy(d).start()

    if fused:
        greet(late_sem, 0, layer_first * fsdp_size)

    @pl.when(me_s == seq_size - 1)
    def _():
        sg_v[pl.ds(rows, LF), :] = jnp.zeros((LF, chans), BF16)

    for load in loads[2:5]:
        load.wait()

    def scale(b, c):
        lanes = lanes_of(b)
        new = (og_v[rest, lanes].astype(F32) * gate_v[rest, lanes].astype(F32)).astype(BF16)
        sg_v[rest, lanes] = new
        terms = jnp.sum(new.astype(F32) * x_v[rest, lanes].astype(F32), axis=0, keepdims=True)
        terms = terms + jnp.sum(
            sg_v[rim, lanes].astype(F32) * x_v[rim, lanes].astype(F32), axis=0, keepdims=True)
        bias_v[pl.ds(b, 1), :] = terms
        return c

    lax.fori_loop(0, blocks, scale, 0, unroll=2)

    row_at = lax.broadcasted_iota(jnp.int32, (LF, LANES), 0)
    lane_at = lax.broadcasted_iota(jnp.int32, (LF, LANES), 1)
    above = lane_at >= row_at

    def windows(p, lanes):
        at = 2 * LF * p
        return jnp.concatenate(
            [sg_v[at:at + 2 * LF, lanes], sg_v[at + LF:at + 3 * LF, lanes]], axis=1)

    def split_groups(both):
        lane = lax.broadcasted_iota(jnp.int32, both.shape, 1)
        owner = lax.rem(lax.div(lane, GS), PER)
        return jnp.concatenate(
            [both * (owner == g).astype(F32).astype(BF16) for g in range(PER)], axis=0)

    def products(left, right):
        return lax.dot_general(
            split_groups(left), right, (((1,), (1,)), ((), ())), preferred_element_type=F32)

    def fold(wrapped):
        parts = [wrapped[:8]] + [
            pltpu.roll(wrapped[8 * k:8 * k + 8], LANES - 8 * k, 1) for k in range(1, LF // 8)]
        while len(parts) > 1:
            parts = [one + two for one, two in zip(parts[::2], parts[1::2])]
        return parts[0]

    sub = lax.broadcasted_iota(jnp.int32, (8, LANES), 0)

    def diagonals(wholes):
        for bit in (2, 1, 0):
            step = 1 << bit
            odd = lax.rem(lax.div(sub, step), 2) == 1
            wholes = [
                jnp.where(odd, pltpu.roll(wholes[i + step], step, 0), wholes[i])
                + pltpu.roll(
                    jnp.where(odd, wholes[i + step], pltpu.roll(wholes[i], 8 - step, 0)),
                    LANES - step, 1)
                for i in range(step)]
        return wholes[0]

    def correlate(b):
        lanes = lanes_of(b)
        left = jnp.concatenate([x_v[at:at + LF, lanes] for at in range(0, rows, LF)], axis=1)
        right = jnp.concatenate(
            [sg_v[at:at + 2 * LF, lanes] for at in range(0, rows, LF)], axis=1)
        prod = products(left, right)
        wholes = []
        for g in range(PER):
            one = prod[g * LF:(g + 1) * LF]
            wholes.append(fold(jnp.where(above, one[:, :LANES], one[:, LANES:])))
        part_v[pl.ds(pl.multiple_of(b * PER, PER), PER), :] = diagonals(wholes)

    def correlate_two(i, c):
        @pl.when(me_s < seq_size - 1)
        def _():
            lanes = pl.ds(pl.multiple_of(i * 2 * LANES, 2 * LANES), 2 * LANES)
            pltpu.make_async_remote_copy(
                src_ref=sg_v.at[rim, lanes], dst_ref=sg_v.at[pl.ds(rows, LF), lanes],
                send_sem=halo_send, recv_sem=halo_recv.at[i],
                device_id=(me_s + 1, me_f), device_id_type=MESH).wait_recv()

        correlate(2 * i)
        correlate(2 * i + 1)
        return c

    def build(b, c):
        first = lax.rem(me_f, sharing) * groups + b * PER
        taps = taps_v[pl.ds(pl.multiple_of(first, PER), PER), :]
        for g in range(PER):
            band = pltpu.roll(
                jnp.broadcast_to(taps[g:g + 1], (LF, LANES)), 0, 1, stride=1, stride_axis=0)
            zero = jnp.zeros_like(band)
            toep_v[b, g * LF:(g + 1) * LF, :LANES] = jnp.where(above, band, zero).astype(BF16)
            toep_v[b, g * LF:(g + 1) * LF, LANES:] = jnp.where(above, zero, band).astype(BF16)
        return c

    def conv(b, c, p):
        lanes = lanes_of(b)
        at = 2 * LF * p
        prod = jnp.dot(toep_v[b], windows(p, lanes), preferred_element_type=F32)
        owner = lax.div(lax.broadcasted_iota(jnp.int32, (LF, 2 * LANES), 1), GS)
        owner = lax.rem(owner, PER)
        out = prod[:LF]
        for g in range(1, PER):
            out = jnp.where(owner == g, prod[g * LF:(g + 1) * LF], out)
        skip = skip_ref[pl.ds(b, 1), :]
        for half in range(2):
            here = slice(at + half * LF, at + (half + 1) * LF)
            direct = skip * sg_v[here, lanes].astype(F32)
            out_v[here, lanes] = (
                out[:, half * LANES:(half + 1) * LANES] + direct).astype(BF16)
        return c

    lax.fori_loop(0, blocks // 2, correlate_two, 0)

    if fused:
        half_taps = width // 2
        pack_v[:groups, :] = part_v[...]
        pack_v[groups:, :] = pltpu.roll(part_v[...], LANES - half_taps, 1)
        turned = pack_v[...].T.astype(BF16)
        high = bias_v[...].astype(BF16)
        low = (bias_v[...] - high.astype(F32)).astype(BF16)
        both_parts = jnp.concatenate([high, low], axis=0)
        for f in range(fsdp_size):
            send_v[f, :half_taps, :] = turned[f * width:f * width + half_taps]
            send_v[f, half_taps:, :] = both_parts

        slot = (fsdp_size + 1) * half_taps

        def term_rows(o_s, d_f):
            at = o_s * slot + (0 if d_f == 0 else (d_f + 1) * half_taps)
            return pl.ds(pl.multiple_of(at, half_taps), half_taps * (2 if d_f == 0 else 1))

        recv_v[term_rows(me_s, 0), :] = send_v[me_f]

        @pl.when(layer_end < seq_size)
        def _():
            pl.semaphore_wait(late_sem, (seq_size - layer_end) * fsdp_size)

        def term_copy(o_s, d_f):
            o_f = lax.rem(me_f + d_f, fsdp_size)
            back = (fsdp_size - d_f) % fsdp_size
            return pltpu.make_async_remote_copy(
                src_ref=send_v.at[o_f, pl.ds(0, half_taps * (2 if d_f == 0 else 1))],
                dst_ref=recv_v.at[term_rows(me_s, back)],
                send_sem=term_send, recv_sem=term_recv,
                device_id=(o_s, o_f), device_id_type=MESH)

        upper = lax.div(me_s, seq_size // 2)

        def send_terms(i, c):
            mine = upper * me_s + (1 - upper) * (seq_size - 1 - me_s)
            at = i + lax.div(i + seq_size - mine, seq_size)
            o_s = upper * at + (1 - upper) * (seq_size - 1 - at)
            for d_f in range(fsdp_size):
                term_copy(o_s, d_f).start()
            return c

        lax.fori_loop(0, seq_size - 1, send_terms, 0)
        for d_f in range(1, fsdp_size):
            term_copy(me_s, d_f).start()

    loads[5].wait()
    loads[6].wait()
    for d in range(1, fsdp_size):
        tap_arrival(d).wait_recv()
    taps_v[...] = taps_r[...].T
    lax.fori_loop(0, blocks, build, 0, unroll=2)

    def out_copy(p):
        span = pl.ds(2 * LF * p, 2 * LF)
        return pltpu.make_async_copy(out_v.at[span], ig_hbm.at[span], out_sem.at[p])

    for p in range(pairs):
        lax.fori_loop(0, blocks, functools.partial(conv, p=p), 0, unroll=2)
        out_copy(p).start()

    for d in range(1, fsdp_size):
        tap_copy(d).wait_send()

    @pl.when(me_s > 0)
    def _():
        halo_copy(me_s - 1, 0, blocks).wait_send()

    if fused:
        whole = recv_v.at[pl.ds(0, seq_size * slot - 2 * half_taps)]
        every = pltpu.make_async_remote_copy(
            src_ref=whole, dst_ref=whole, send_sem=term_send, recv_sem=term_recv,
            device_id=(lax.rem(me_s + 1, seq_size), me_f), device_id_type=MESH)
        every.wait_send()
        every.wait_recv()
        lane = lax.broadcasted_iota(jnp.int32, (half_taps, LANES), 1)
        for d_f in range(fsdp_size):
            piece = recv_v[term_rows(0, d_f), :].astype(F32)
            for k in range(1, seq_size):
                piece = piece + recv_v[term_rows(k, d_f), :].astype(F32)
            if d_f == 0:
                bias_ref[...] = (
                    piece[half_taps:half_taps + blocks] + piece[half_taps + blocks:])
                piece = piece[:half_taps]
            sums_v[lax.rem(me_f + d_f, fsdp_size)] = piece
        for f in range(0, fsdp_size, 2):
            pair = pl.ds(f * groups, 2 * groups)
            fg_ref[:half_taps, pair] = jnp.where(
                lane < groups, sums_v[f], pltpu.roll(sums_v[f + 1], groups, 1))
            fg_ref[half_taps:, pair] = jnp.where(
                lane < groups, pltpu.roll(sums_v[f], groups, 1), sums_v[f + 1])
    else:
        fg_ref[...] = part_v[...]
        bias_ref[...] = bias_v[...]
    for p in range(pairs):
        out_copy(p).wait()


def writer(*refs):
    count = len(refs) // 2
    sources, targets, sems = refs[:count], refs[count:2 * count], refs[2 * count]
    copies = [
        pltpu.make_async_copy(a, b, sems.at[i]) for i, (a, b) in enumerate(zip(sources, targets))]
    for copy in copies:
        copy.start()
    for copy in copies:
        copy.wait()


def write_out(*arrays):
    return pl.pallas_call(
        writer,
        out_shape=tuple(pltpu.HBM(a.shape, a.dtype) for a in arrays),
        in_specs=[pl.BlockSpec(memory_space=pltpu.VMEM)] * len(arrays),
        out_specs=(pl.BlockSpec(memory_space=pltpu.HBM),) * len(arrays),
        scratch_shapes=[pltpu.SemaphoreType.DMA((len(arrays),))],
    )(*(pltpu.with_memory_space_constraint(a, pltpu.VMEM) for a in arrays))


def on_device(seq_size, fsdp_size, conv_input, gate, out_grad, filters, skip_bias):
    rows, chans = conv_input.shape
    blocks = chans // LANES
    groups = chans // GS
    width = LF // fsdp_size
    fused = (
        seq_size % LAYER == 0 and seq_size <= 8 and fsdp_size % 2 == 0
        and 2 * groups == LANES and 2 * blocks == width // 2)
    seq_terms = seq_size if fused else 1
    fg_shape = (width, fsdp_size * groups) if fused else (groups, LF)
    term_rows = width if fused else 32
    hbm_spec = pl.BlockSpec(memory_space=pltpu.HBM)
    vmem_spec = pl.BlockSpec(memory_space=pltpu.VMEM)
    dma = pltpu.SemaphoreType.DMA
    input_grad, filter_part, bias_part = pl.pallas_call(
        functools.partial(kernel, seq_size, fsdp_size, fused),
        out_shape=(
            jax.ShapeDtypeStruct((rows, chans), BF16),
            jax.ShapeDtypeStruct(fg_shape, F32),
            jax.ShapeDtypeStruct((blocks, LANES), F32),
        ),
        in_specs=[hbm_spec] * 5,
        out_specs=(hbm_spec, vmem_spec, vmem_spec),
        scratch_shapes=[
            pltpu.VMEM((blocks, LANES), F32),
            pltpu.VMEM((rows, chans), BF16),
            pltpu.VMEM((rows, chans), BF16),
            pltpu.VMEM((rows, chans), BF16),
            pltpu.VMEM((rows + LF, chans), BF16),
            pltpu.VMEM((rows, chans), BF16),
            pltpu.VMEM((blocks, PER * LF, 2 * LANES), BF16),
            pltpu.VMEM((LF, LANES), F32),
            pltpu.VMEM((LANES, LF), F32),
            pltpu.VMEM((groups, LANES), F32),
            pltpu.VMEM((blocks, LANES), F32),
            pltpu.VMEM((2 * groups, LANES), F32),
            pltpu.VMEM((fsdp_size, term_rows, LANES), BF16),
            pltpu.VMEM((seq_terms * (fsdp_size + 1) * (term_rows // 2), LANES), BF16),
            pltpu.VMEM((fsdp_size, term_rows // 2, LANES), F32),
            dma((7,)),
            dma((rows // (2 * LF),)),
            dma,
            dma((blocks // 2,)),
            dma((fsdp_size,)),
            dma((fsdp_size,)),
            pltpu.SemaphoreType.REGULAR,
            dma,
            dma,
        ],
        compiler_params=pltpu.CompilerParams(
            collective_id=0, has_side_effects=True, vmem_limit_bytes=VMEM_GRANT),
    )(*(pltpu.with_memory_space_constraint(a, pltpu.HBM) for a in (
        conv_input, gate, out_grad, filters.T, skip_bias.reshape(blocks, LANES))))
    if fused:
        input_grad, filter_part, bias_part = write_out(input_grad, filter_part, bias_part)
        return input_grad, filter_part.T, bias_part.reshape(chans)
    spread = lax.all_to_all(
        filter_part, "fsdp", split_axis=1, concat_axis=0, tiled=True)
    filter_grad, bias_grad = lax.psum((spread, bias_part.reshape(chans)), "seq")
    return input_grad, filter_grad, bias_grad


def solution(mesh):
    placed = (P("seq", "fsdp"), P("seq", "fsdp"), P("seq", "fsdp"), P(None, "fsdp"), P("fsdp"))
    return jax.shard_map(
        functools.partial(on_device, mesh.shape["seq"], mesh.shape["fsdp"]),
        mesh=mesh,
        in_specs=placed,
        out_specs=(P("seq", "fsdp"), P(None, "fsdp"), P("fsdp")),
        check_vma=False,
    )
```

```python
import functools

import jax
import jax.numpy as jnp
from jax import lax
from jax.experimental import pallas as pl
from jax.experimental.pallas import tpu as pltpu
from jax.sharding import PartitionSpec as P

GS = 16
VMEM_GRANT = 105 << 19
LF = 128
LANES = 128
PER = LANES // GS
MESH = pl.DeviceIdType.MESH
F32 = jnp.float32
BF16 = jnp.bfloat16


def kernel(
    seq_size, fsdp_size, fused,
    x_hbm, gate_hbm, og_hbm, filt_hbm, skip_hbm,
    ig_ref, fg_ref, bias_ref,
    skip_ref, x_v, gate_v, og_v, sg_v, toep_v, taps_r, taps_v, part_v, bias_v,
    pack_v, send_v, recv_v, bias_r,
    load_sem, halo_send, halo_recv, tap_send, tap_recv, row_sem, late_sem, term_send, term_recv, bias_send, bias_recv,
):
    rows, chans = x_v.shape
    blocks = chans // LANES
    pairs = rows // (2 * LF)
    groups = chans // GS
    me_s = lax.axis_index("seq")
    me_f = lax.axis_index("fsdp")

    width = LF // fsdp_size
    sharing = LANES // groups

    def tap_lanes(owner):
        return pl.ds(pl.multiple_of(lax.div(owner, sharing) * LANES, LANES), LANES)

    def tap_rows(source):
        return pl.ds(pl.multiple_of(source * width, 8), width)

    rim = pl.ds(0, LF)
    rest = pl.ds(LF, rows - LF)
    loads = [
        pltpu.make_async_copy(og_hbm.at[rim], og_v.at[rim], load_sem.at[0]),
        pltpu.make_async_copy(gate_hbm.at[rim], gate_v.at[rim], load_sem.at[1]),
        pltpu.make_async_copy(og_hbm.at[rest], og_v.at[rest], load_sem.at[2]),
        pltpu.make_async_copy(gate_hbm.at[rest], gate_v.at[rest], load_sem.at[3]),
        pltpu.make_async_copy(x_hbm, x_v, load_sem.at[4]),
        pltpu.make_async_copy(
            filt_hbm.at[:, tap_lanes(me_f)], taps_r.at[tap_rows(me_f)], load_sem.at[5]),
        pltpu.make_async_copy(skip_hbm, skip_ref, load_sem.at[6]),
    ]
    barrier = pltpu.get_barrier_semaphore()
    def greet(semaphore, first, end):
        def step(other, c):
            o_s, o_f = lax.div(other, fsdp_size), lax.rem(other, fsdp_size)
            pl.semaphore_signal(
                semaphore, inc=1, device_id=(o_s, o_f), device_id_type=MESH)
            return c

        lax.fori_loop(first, end, step, 0)

    if fused:
        me = me_s * fsdp_size + me_f
        total = seq_size * fsdp_size
        greet(barrier, me_s * fsdp_size, me)
        greet(barrier, me + 1, (me_s + 1) * fsdp_size)
    else:
        for d in range(1, fsdp_size):
            pl.semaphore_signal(
                barrier, inc=1, device_id=(me_s, lax.rem(me_f + d, fsdp_size)),
                device_id_type=MESH)

        @pl.when(me_s > 0)
        def _():
            pl.semaphore_signal(
                barrier, inc=1, device_id=(me_s - 1, me_f), device_id_type=MESH)

        @pl.when(me_s < seq_size - 1)
        def _():
            pl.semaphore_signal(
                barrier, inc=1, device_id=(me_s + 1, me_f), device_id_type=MESH)

    for load in loads:
        load.start()
    if fused:
        def greet_later(o_s, c):
            pl.semaphore_signal(barrier, inc=1, device_id=(o_s, me_f), device_id_type=MESH)
            return c

        lax.fori_loop(me_s + 1, seq_size, greet_later, 0)
    loads[0].wait()
    loads[1].wait()
    sg_v[rim, :] = (og_v[rim, :].astype(F32) * gate_v[rim, :].astype(F32)).astype(BF16)

    if fused:
        pl.semaphore_wait(barrier, me_s + fsdp_size - 1)
    else:
        pl.semaphore_wait(barrier, fsdp_size - 1)

        @pl.when(me_s > 0)
        def _():
            pl.semaphore_wait(barrier, 1)

        @pl.when(me_s < seq_size - 1)
        def _():
            pl.semaphore_wait(barrier, 1)

    def lanes_of(b):
        return pl.ds(pl.multiple_of(b * LANES, LANES), LANES)

    def halo_copy(target, first, end):
        lanes = pl.ds(first * LANES, (end - first) * LANES)
        return pltpu.make_async_remote_copy(
            src_ref=sg_v.at[rim, lanes], dst_ref=sg_v.at[pl.ds(rows, LF), lanes],
            send_sem=halo_send, recv_sem=halo_recv.at[first // 2],
            device_id=(target, me_f), device_id_type=MESH)

    @pl.when(me_s > 0)
    def _():
        for b in range(0, blocks, 2):
            halo_copy(me_s - 1, b, b + 2).start()

    def tap_copy(d):
        other = lax.rem(me_f + d, fsdp_size)
        return pltpu.make_async_remote_copy(
            src_ref=filt_hbm.at[:, tap_lanes(other)],
            dst_ref=taps_r.at[tap_rows(me_f)],
            send_sem=tap_send.at[other], recv_sem=tap_recv.at[me_f],
            device_id=(me_s, other), device_id_type=MESH)

    def tap_arrival(d):
        other = lax.rem(me_f + d, fsdp_size)
        return pltpu.make_async_remote_copy(
            src_ref=filt_hbm.at[:, tap_lanes(other)],
            dst_ref=taps_r.at[tap_rows(other)],
            send_sem=tap_send.at[other], recv_sem=tap_recv.at[other],
            device_id=(me_s, other), device_id_type=MESH)

    for d in range(1, fsdp_size):
        tap_copy(d).start()

    if fused:
        greet(row_sem, me_s * fsdp_size, me)
        greet(row_sem, me + 1, (me_s + 1) * fsdp_size)

    @pl.when(me_s == seq_size - 1)
    def _():
        sg_v[pl.ds(rows, LF), :] = jnp.zeros((LF, chans), BF16)

    for load in loads[2:5]:
        load.wait()

    def scale(b, c):
        lanes = lanes_of(b)
        new = (og_v[rest, lanes].astype(F32) * gate_v[rest, lanes].astype(F32)).astype(BF16)
        sg_v[rest, lanes] = new
        terms = jnp.sum(new.astype(F32) * x_v[rest, lanes].astype(F32), axis=0, keepdims=True)
        terms = terms + jnp.sum(
            sg_v[rim, lanes].astype(F32) * x_v[rim, lanes].astype(F32), axis=0, keepdims=True)
        bias_v[pl.ds(b, 1), :] = terms
        return c

    lax.fori_loop(0, blocks, scale, 0, unroll=2)

    if fused:
        def bias_copy(o_s):
            return pltpu.make_async_remote_copy(
                src_ref=bias_v, dst_ref=bias_r.at[me_s], send_sem=bias_send, recv_sem=bias_recv,
                device_id=(o_s, me_f), device_id_type=MESH)

        def send_bias(first, end):
            def step(o_s, c):
                bias_copy(o_s).start()
                return c

            lax.fori_loop(first, end, step, 0)

        send_bias(0, me_s)

    row_at = lax.broadcasted_iota(jnp.int32, (LF, LANES), 0)
    lane_at = lax.broadcasted_iota(jnp.int32, (LF, LANES), 1)
    above = lane_at >= row_at

    def windows(p, lanes):
        at = 2 * LF * p
        return jnp.concatenate(
            [sg_v[at:at + 2 * LF, lanes], sg_v[at + LF:at + 3 * LF, lanes]], axis=1)

    def split_groups(both):
        lane = lax.broadcasted_iota(jnp.int32, both.shape, 1)
        owner = lax.rem(lax.div(lane, GS), PER)
        return jnp.concatenate(
            [both * (owner == g).astype(F32).astype(BF16) for g in range(PER)], axis=0)

    def products(left, right):
        return lax.dot_general(
            split_groups(left), right, (((1,), (1,)), ((), ())), preferred_element_type=F32)

    def fold(wrapped):
        parts = [wrapped[:8]] + [
            pltpu.roll(wrapped[8 * k:8 * k + 8], LANES - 8 * k, 1) for k in range(1, LF // 8)]
        while len(parts) > 1:
            parts = [one + two for one, two in zip(parts[::2], parts[1::2])]
        return parts[0]

    sub = lax.broadcasted_iota(jnp.int32, (8, LANES), 0)

    def diagonals(wholes):
        for bit in (2, 1, 0):
            step = 1 << bit
            odd = lax.rem(lax.div(sub, step), 2) == 1
            wholes = [
                jnp.where(odd, pltpu.roll(wholes[i + step], step, 0), wholes[i])
                + pltpu.roll(
                    jnp.where(odd, wholes[i + step], pltpu.roll(wholes[i], 8 - step, 0)),
                    LANES - step, 1)
                for i in range(step)]
        return wholes[0]

    def tiles(ref, lanes, span, count):
        return jnp.concatenate([ref[at:at + span, lanes] for at in range(0, count * LF, LF)], axis=1)

    def correlate(b):
        lanes = lanes_of(b)
        prod = products(
            tiles(x_v, lanes, LF, rows // LF), tiles(sg_v, lanes, 2 * LF, rows // LF))
        wholes = []
        for g in range(PER):
            one = prod[g * LF:(g + 1) * LF]
            wholes.append(fold(jnp.where(above, one[:, :LANES], one[:, LANES:])))
        part_v[pl.ds(pl.multiple_of(b * PER, PER), PER), :] = diagonals(wholes)

    def correlate_own(b):
        lanes = lanes_of(b)
        last = jnp.concatenate(
            [sg_v[rows - LF:rows, lanes], jnp.zeros((LF, LANES), BF16)], axis=0)
        prod = products(
            tiles(x_v, lanes, LF, rows // LF),
            jnp.concatenate([tiles(sg_v, lanes, 2 * LF, rows // LF - 1), last], axis=1))
        wholes = []
        for g in range(PER):
            one = prod[g * LF:(g + 1) * LF]
            wholes.append(fold(jnp.where(above, one[:, :LANES], one[:, LANES:])))
        part_v[b * PER:(b + 1) * PER, :] = diagonals(wholes)

    def correlate_next(b):
        lanes = lanes_of(b)
        prod = products(x_v[rows - LF:rows, lanes], sg_v[rows:rows + LF, lanes])
        wholes = []
        for g in range(PER):
            one = prod[g * LF:(g + 1) * LF]
            wholes.append(fold(jnp.where(above, jnp.zeros_like(one), one)))
        return diagonals(wholes)

    def halo_arrival(i):
        @pl.when(me_s < seq_size - 1)
        def _():
            lanes = pl.ds(pl.multiple_of(i * 2 * LANES, 2 * LANES), 2 * LANES)
            pltpu.make_async_remote_copy(
                src_ref=sg_v.at[rim, lanes], dst_ref=sg_v.at[pl.ds(rows, LF), lanes],
                send_sem=halo_send, recv_sem=halo_recv.at[i],
                device_id=(me_s + 1, me_f), device_id_type=MESH).wait_recv()

    def correlate_two(i, c):
        halo_arrival(i)
        correlate(2 * i)
        correlate(2 * i + 1)
        return c

    def build(b):
        first = lax.rem(me_f, sharing) * groups + b * PER
        taps = taps_v[pl.ds(pl.multiple_of(first, PER), PER), :]
        for g in range(PER):
            band = pltpu.roll(
                jnp.broadcast_to(taps[g:g + 1], (LF, LANES)), 0, 1, stride=1, stride_axis=0)
            zero = jnp.zeros_like(band)
            toep_v[b, g * LF:(g + 1) * LF, :LANES] = jnp.where(above, band, zero).astype(BF16)
            toep_v[b, g * LF:(g + 1) * LF, LANES:] = jnp.where(above, zero, band).astype(BF16)

    def conv(b, p):
        lanes = lanes_of(b)
        at = 2 * LF * p
        prod = jnp.dot(toep_v[b], windows(p, lanes), preferred_element_type=F32)
        owner = lax.div(lax.broadcasted_iota(jnp.int32, (LF, 2 * LANES), 1), GS)
        owner = lax.rem(owner, PER)
        out = prod[:LF]
        for g in range(1, PER):
            out = jnp.where(owner == g, prod[g * LF:(g + 1) * LF], out)
        skip = skip_ref[pl.ds(b, 1), :]
        for half in range(2):
            here = slice(at + half * LF, at + (half + 1) * LF)
            direct = skip * sg_v[here, lanes].astype(F32)
            ig_ref[here, lanes] = (
                out[:, half * LANES:(half + 1) * LANES] + direct).astype(BF16)

    correlate_own(blocks - 2)
    correlate_own(blocks - 1)
    if fused:
        pl.semaphore_wait(row_sem, fsdp_size - 1)
        greet(late_sem, 0, me_s * fsdp_size)

    lax.fori_loop(0, blocks // 2 - 1, correlate_two, 0)

    if fused:
        @pl.when(me_s < seq_size - 1)
        def _():
            pl.semaphore_wait(late_sem, (seq_size - 1 - me_s) * fsdp_size)

        send_bias(me_s + 1, seq_size)

    halo_arrival(blocks // 2 - 1)
    here = pl.ds(groups - 2 * PER, 2 * PER)
    part_v[here, :] = part_v[here, :] + jnp.concatenate(
        [correlate_next(blocks - 2), correlate_next(blocks - 1)], axis=0)

    if fused:
        half_taps = width // 2
        pack_v[:groups, :] = part_v[...]
        pack_v[groups:, :] = pltpu.roll(part_v[...], LANES - half_taps, 1)
        turned = pack_v[...].T.astype(BF16)
        for f in range(fsdp_size):
            send_v[f] = turned[f * width:f * width + half_taps]
        recv_v[me] = send_v[me_f]

        def send_terms(other, c):
            o_s, o_f = lax.div(other, fsdp_size), lax.rem(other, fsdp_size)
            pltpu.make_async_remote_copy(
                src_ref=send_v.at[o_f], dst_ref=recv_v.at[me],
                send_sem=term_send, recv_sem=term_recv,
                device_id=(o_s, o_f), device_id_type=MESH).start()
            return c

        lax.fori_loop(0, me, send_terms, 0)
        lax.fori_loop(me + 1, total, send_terms, 0)

    loads[5].wait()
    loads[6].wait()
    for d in range(1, fsdp_size):
        tap_arrival(d).wait_recv()
    taps_v[...] = taps_r[...].T

    def build_conv(b, c):
        build(b)
        for p in range(pairs):
            conv(b, p)
        return c

    lax.fori_loop(0, blocks, build_conv, 0, unroll=2)

    for d in range(1, fsdp_size):
        tap_copy(d).wait_send()

    @pl.when(me_s > 0)
    def _():
        halo_copy(me_s - 1, 0, blocks).wait_send()

    if fused:
        def every(ref, slots, send_sem, recv_sem):
            span = ref.at[pl.ds(0, slots)]
            return pltpu.make_async_remote_copy(
                src_ref=span, dst_ref=span, send_sem=send_sem, recv_sem=recv_sem,
                device_id=(lax.rem(me_s + 1, seq_size), me_f), device_id_type=MESH)

        biases = every(bias_r, seq_size - 1, bias_send, bias_recv)
        biases.wait_send()
        biases.wait_recv()
        bias_r[me_s] = bias_v[...]
        bias_total = bias_r[0]
        for k in range(1, seq_size):
            bias_total = bias_total + bias_r[k]
        bias_ref[...] = bias_total
        terms = every(recv_v, total - 1, term_send, term_recv)
        terms.wait_send()
        terms.wait_recv()
        lane = lax.broadcasted_iota(jnp.int32, (half_taps, LANES), 1)
        sums = []
        for f in range(fsdp_size):
            piece = recv_v[f].astype(F32)
            for k in range(1, seq_size):
                piece = piece + recv_v[k * fsdp_size + f].astype(F32)
            sums.append(piece)
        for f in range(0, fsdp_size, 2):
            pair = pl.ds(f * groups, 2 * groups)
            fg_ref[:half_taps, pair] = jnp.where(
                lane < groups, sums[f], pltpu.roll(sums[f + 1], groups, 1))
            fg_ref[half_taps:, pair] = jnp.where(
                lane < groups, pltpu.roll(sums[f], groups, 1), sums[f + 1])
    else:
        fg_ref[...] = part_v[...]
        bias_ref[...] = bias_v[...]


def writer(*refs):
    count = len(refs) // 2
    sources, targets, sems = refs[:count], refs[count:2 * count], refs[2 * count]
    copies = [
        pltpu.make_async_copy(a, b, sems.at[i]) for i, (a, b) in enumerate(zip(sources, targets))]
    for copy in copies:
        copy.start()
    for copy in copies:
        copy.wait()


def write_out(*arrays):
    return pl.pallas_call(
        writer,
        out_shape=tuple(pltpu.HBM(a.shape, a.dtype) for a in arrays),
        in_specs=[pl.BlockSpec(memory_space=pltpu.VMEM)] * len(arrays),
        out_specs=(pl.BlockSpec(memory_space=pltpu.HBM),) * len(arrays),
        scratch_shapes=[pltpu.SemaphoreType.DMA((len(arrays),))],
    )(*(pltpu.with_memory_space_constraint(a, pltpu.VMEM) for a in arrays))


def on_device(seq_size, fsdp_size, conv_input, gate, out_grad, filters, skip_bias):
    rows, chans = conv_input.shape
    blocks = chans // LANES
    groups = chans // GS
    width = LF // fsdp_size
    fused = (
        seq_size <= 8 and fsdp_size % 2 == 0
        and 2 * groups == LANES)
    everyone = seq_size * fsdp_size if fused else 1
    fg_shape = (width, fsdp_size * groups) if fused else (groups, LF)
    half_taps = width // 2
    hbm_spec = pl.BlockSpec(memory_space=pltpu.HBM)
    vmem_spec = pl.BlockSpec(memory_space=pltpu.VMEM)
    dma = pltpu.SemaphoreType.DMA
    input_grad, filter_part, bias_part = pl.pallas_call(
        functools.partial(kernel, seq_size, fsdp_size, fused),
        out_shape=(
            jax.ShapeDtypeStruct((rows, chans), BF16),
            jax.ShapeDtypeStruct(fg_shape, F32),
            jax.ShapeDtypeStruct((blocks, LANES), F32),
        ),
        in_specs=[hbm_spec] * 5,
        out_specs=(vmem_spec, vmem_spec, vmem_spec),
        scratch_shapes=[
            pltpu.VMEM((blocks, LANES), F32),
            pltpu.VMEM((rows, chans), BF16),
            pltpu.VMEM((rows, chans), BF16),
            pltpu.VMEM((rows, chans), BF16),
            pltpu.VMEM((rows + LF, chans), BF16),
            pltpu.VMEM((blocks, PER * LF, 2 * LANES), BF16),
            pltpu.VMEM((LF, LANES), F32),
            pltpu.VMEM((LANES, LF), F32),
            pltpu.VMEM((groups, LANES), F32),
            pltpu.VMEM((blocks, LANES), F32),
            pltpu.VMEM((2 * groups, LANES), F32),
            pltpu.VMEM((fsdp_size, half_taps, LANES), BF16),
            pltpu.VMEM((everyone, half_taps, LANES), BF16),
            pltpu.VMEM((everyone // fsdp_size if fused else 1, blocks, LANES), F32),
            dma((7,)),
            dma,
            dma((blocks // 2,)),
            dma((fsdp_size,)),
            dma((fsdp_size,)),
            pltpu.SemaphoreType.REGULAR,
            pltpu.SemaphoreType.REGULAR,
            dma,
            dma,
            dma,
            dma,
        ],
        compiler_params=pltpu.CompilerParams(
            collective_id=0, has_side_effects=True, vmem_limit_bytes=VMEM_GRANT),
    )(*(pltpu.with_memory_space_constraint(a, pltpu.HBM) for a in (
        conv_input, gate, out_grad, filters.T, skip_bias.reshape(blocks, LANES))))
    if fused:
        input_grad, filter_part, bias_part = write_out(input_grad, filter_part, bias_part)
        return input_grad, filter_part.T, bias_part.reshape(chans)
    spread = lax.all_to_all(
        filter_part, "fsdp", split_axis=1, concat_axis=0, tiled=True)
    filter_grad, bias_grad = lax.psum((spread, bias_part.reshape(chans)), "seq")
    return input_grad, filter_grad, bias_grad


def solution(mesh):
    placed = (P("seq", "fsdp"), P("seq", "fsdp"), P("seq", "fsdp"), P(None, "fsdp"), P("fsdp"))
    return jax.shard_map(
        functools.partial(on_device, mesh.shape["seq"], mesh.shape["fsdp"]),
        mesh=mesh,
        in_specs=placed,
        out_specs=(P("seq", "fsdp"), P(None, "fsdp"), P("fsdp")),
        check_vma=False,
    )
```

```python
import functools

import jax
import jax.numpy as jnp
from jax import lax
from jax.experimental import pallas as pl
from jax.experimental.pallas import tpu as pltpu
from jax.sharding import PartitionSpec as P

GS = 16
VMEM_GRANT = 105 << 19
LF = 128
LANES = 128
PER = LANES // GS
MESH = pl.DeviceIdType.MESH
F32 = jnp.float32
BF16 = jnp.bfloat16


def kernel(
    seq_size, fsdp_size, fused,
    x_hbm, gate_hbm, og_hbm, filt_hbm, skip_hbm,
    ig_ref, fg_ref, bias_ref,
    skip_ref, x_v, gate_v, og_v, sg_v, toep_v, taps_r, taps_v, part_v, bias_v,
    pack_v, send_v, recv_v, bias_r,
    load_sem, halo_send, halo_recv, tap_send, tap_recv, row_sem, late_sem, all_sem, term_send, term_recv, bias_send, bias_recv,
):
    rows, chans = x_v.shape
    blocks = chans // LANES
    pairs = rows // (2 * LF)
    groups = chans // GS
    me_s = lax.axis_index("seq")
    me_f = lax.axis_index("fsdp")

    width = LF // fsdp_size
    sharing = LANES // groups

    def tap_lanes(owner):
        return pl.ds(pl.multiple_of(lax.div(owner, sharing) * LANES, LANES), LANES)

    def tap_rows(source):
        return pl.ds(pl.multiple_of(source * width, 8), width)

    rim = pl.ds(0, LF)
    rest = pl.ds(LF, rows - LF)
    loads = [
        pltpu.make_async_copy(og_hbm.at[rim], og_v.at[rim], load_sem.at[0]),
        pltpu.make_async_copy(gate_hbm.at[rim], gate_v.at[rim], load_sem.at[1]),
        pltpu.make_async_copy(og_hbm.at[rest], og_v.at[rest], load_sem.at[2]),
        pltpu.make_async_copy(gate_hbm.at[rest], gate_v.at[rest], load_sem.at[3]),
        pltpu.make_async_copy(x_hbm, x_v, load_sem.at[4]),
        pltpu.make_async_copy(
            filt_hbm.at[:, tap_lanes(me_f)], taps_r.at[tap_rows(me_f)], load_sem.at[5]),
        pltpu.make_async_copy(skip_hbm, skip_ref, load_sem.at[6]),
    ]
    barrier = pltpu.get_barrier_semaphore()
    def greet(semaphore, first, end):
        def step(other, c):
            o_s, o_f = lax.div(other, fsdp_size), lax.rem(other, fsdp_size)
            pl.semaphore_signal(
                semaphore, inc=1, device_id=(o_s, o_f), device_id_type=MESH)
            return c

        lax.fori_loop(first, end, step, 0)

    if fused:
        me = me_s * fsdp_size + me_f
        total = seq_size * fsdp_size
        row = me_s * fsdp_size
        row_end = row + fsdp_size

        def greet_column(semaphore, first, end):
            def step(o_s, c):
                pl.semaphore_signal(semaphore, inc=1, device_id=(o_s, me_f), device_id_type=MESH)
                return c

            lax.fori_loop(first, end, step, 0)

        greet_column(barrier, me_s + 1, seq_size)
        greet(barrier, me + 1, row_end)
    else:
        for d in range(1, fsdp_size):
            pl.semaphore_signal(
                barrier, inc=1, device_id=(me_s, lax.rem(me_f + d, fsdp_size)),
                device_id_type=MESH)

        @pl.when(me_s > 0)
        def _():
            pl.semaphore_signal(
                barrier, inc=1, device_id=(me_s - 1, me_f), device_id_type=MESH)

        @pl.when(me_s < seq_size - 1)
        def _():
            pl.semaphore_signal(
                barrier, inc=1, device_id=(me_s + 1, me_f), device_id_type=MESH)

    for load in loads:
        load.start()
    loads[0].wait()
    loads[1].wait()
    sg_v[rim, :] = (og_v[rim, :].astype(F32) * gate_v[rim, :].astype(F32)).astype(BF16)

    if fused:
        @pl.when(me_s + me_f > 0)
        def _():
            pl.semaphore_wait(barrier, me_s + me_f)
    else:
        pl.semaphore_wait(barrier, fsdp_size - 1)

        @pl.when(me_s > 0)
        def _():
            pl.semaphore_wait(barrier, 1)

        @pl.when(me_s < seq_size - 1)
        def _():
            pl.semaphore_wait(barrier, 1)

    def lanes_of(b):
        return pl.ds(pl.multiple_of(b * LANES, LANES), LANES)

    def halo_copy(target, first, end):
        lanes = pl.ds(first * LANES, (end - first) * LANES)
        return pltpu.make_async_remote_copy(
            src_ref=sg_v.at[rim, lanes], dst_ref=sg_v.at[pl.ds(rows, LF), lanes],
            send_sem=halo_send, recv_sem=halo_recv.at[first // 2],
            device_id=(target, me_f), device_id_type=MESH)

    @pl.when(me_s > 0)
    def _():
        for b in range(0, blocks, 2):
            halo_copy(me_s - 1, b, b + 2).start()

    def tap_copy(other):
        return pltpu.make_async_remote_copy(
            src_ref=filt_hbm.at[:, tap_lanes(other)],
            dst_ref=taps_r.at[tap_rows(me_f)],
            send_sem=tap_send.at[other], recv_sem=tap_recv.at[me_f],
            device_id=(me_s, other), device_id_type=MESH)

    def tap_arrival(d):
        other = lax.rem(me_f + d, fsdp_size)
        return pltpu.make_async_remote_copy(
            src_ref=filt_hbm.at[:, tap_lanes(other)],
            dst_ref=taps_r.at[tap_rows(other)],
            send_sem=tap_send.at[other], recv_sem=tap_recv.at[other],
            device_id=(me_s, other), device_id_type=MESH)

    def send_taps(first, end):
        def step(other, c):
            tap_copy(other).start()
            return c

        lax.fori_loop(first, end, step, 0)

    if fused:
        greet(row_sem, row, me)
        greet_column(late_sem, 0, me_s)
    else:
        send_taps(me_f + 1, fsdp_size)
    send_taps(0, me_f)

    @pl.when(me_s == seq_size - 1)
    def _():
        sg_v[pl.ds(rows, LF), :] = jnp.zeros((LF, chans), BF16)

    for load in loads[2:5]:
        load.wait()

    def scale(b, c):
        lanes = lanes_of(b)
        new = (og_v[rest, lanes].astype(F32) * gate_v[rest, lanes].astype(F32)).astype(BF16)
        sg_v[rest, lanes] = new
        terms = jnp.sum(new.astype(F32) * x_v[rest, lanes].astype(F32), axis=0, keepdims=True)
        terms = terms + jnp.sum(
            sg_v[rim, lanes].astype(F32) * x_v[rim, lanes].astype(F32), axis=0, keepdims=True)
        bias_v[pl.ds(b, 1), :] = terms
        return c

    lax.fori_loop(0, blocks, scale, 0, unroll=2)

    if fused:
        def bias_copy(o_s):
            return pltpu.make_async_remote_copy(
                src_ref=bias_v, dst_ref=bias_r.at[me_s], send_sem=bias_send, recv_sem=bias_recv,
                device_id=(o_s, me_f), device_id_type=MESH)

        def send_bias(first, end):
            def step(o_s, c):
                bias_copy(o_s).start()
                return c

            lax.fori_loop(first, end, step, 0)

        send_bias(0, me_s)

    row_at = lax.broadcasted_iota(jnp.int32, (LF, LANES), 0)
    lane_at = lax.broadcasted_iota(jnp.int32, (LF, LANES), 1)
    above = lane_at >= row_at

    def windows(p, lanes):
        at = 2 * LF * p
        return jnp.concatenate(
            [sg_v[at:at + 2 * LF, lanes], sg_v[at + LF:at + 3 * LF, lanes]], axis=1)

    def split_groups(both):
        lane = lax.broadcasted_iota(jnp.int32, both.shape, 1)
        owner = lax.rem(lax.div(lane, GS), PER)
        return jnp.concatenate(
            [both * (owner == g).astype(F32).astype(BF16) for g in range(PER)], axis=0)

    def products(left, right):
        return lax.dot_general(
            split_groups(left), right, (((1,), (1,)), ((), ())), preferred_element_type=F32)

    def fold(wrapped):
        parts = [wrapped[:8]] + [
            pltpu.roll(wrapped[8 * k:8 * k + 8], LANES - 8 * k, 1) for k in range(1, LF // 8)]
        while len(parts) > 1:
            parts = [one + two for one, two in zip(parts[::2], parts[1::2])]
        return parts[0]

    sub = lax.broadcasted_iota(jnp.int32, (8, LANES), 0)

    def diagonals(wholes):
        for bit in (2, 1, 0):
            step = 1 << bit
            odd = lax.rem(lax.div(sub, step), 2) == 1
            wholes = [
                jnp.where(odd, pltpu.roll(wholes[i + step], step, 0), wholes[i])
                + pltpu.roll(
                    jnp.where(odd, wholes[i + step], pltpu.roll(wholes[i], 8 - step, 0)),
                    LANES - step, 1)
                for i in range(step)]
        return wholes[0]

    def tiles(ref, lanes, span, count):
        return jnp.concatenate([ref[at:at + span, lanes] for at in range(0, count * LF, LF)], axis=1)

    def correlate(b):
        lanes = lanes_of(b)
        prod = products(
            tiles(x_v, lanes, LF, rows // LF), tiles(sg_v, lanes, 2 * LF, rows // LF))
        wholes = []
        for g in range(PER):
            one = prod[g * LF:(g + 1) * LF]
            wholes.append(fold(jnp.where(above, one[:, :LANES], one[:, LANES:])))
        part_v[pl.ds(pl.multiple_of(b * PER, PER), PER), :] = diagonals(wholes)

    def correlate_own(b):
        lanes = lanes_of(b)
        last = jnp.concatenate(
            [sg_v[rows - LF:rows, lanes], jnp.zeros((LF, LANES), BF16)], axis=0)
        prod = products(
            tiles(x_v, lanes, LF, rows // LF),
            jnp.concatenate([tiles(sg_v, lanes, 2 * LF, rows // LF - 1), last], axis=1))
        wholes = []
        for g in range(PER):
            one = prod[g * LF:(g + 1) * LF]
            wholes.append(fold(jnp.where(above, one[:, :LANES], one[:, LANES:])))
        part_v[b * PER:(b + 1) * PER, :] = diagonals(wholes)

    def correlate_next(b):
        lanes = lanes_of(b)
        prod = products(x_v[rows - LF:rows, lanes], sg_v[rows:rows + LF, lanes])
        wholes = []
        for g in range(PER):
            one = prod[g * LF:(g + 1) * LF]
            wholes.append(fold(jnp.where(above, jnp.zeros_like(one), one)))
        return diagonals(wholes)

    def halo_arrival(i):
        @pl.when(me_s < seq_size - 1)
        def _():
            lanes = pl.ds(pl.multiple_of(i * 2 * LANES, 2 * LANES), 2 * LANES)
            pltpu.make_async_remote_copy(
                src_ref=sg_v.at[rim, lanes], dst_ref=sg_v.at[pl.ds(rows, LF), lanes],
                send_sem=halo_send, recv_sem=halo_recv.at[i],
                device_id=(me_s + 1, me_f), device_id_type=MESH).wait_recv()

    def correlate_two(i, c):
        halo_arrival(i)
        correlate(2 * i)
        correlate(2 * i + 1)
        return c

    def build(b):
        first = lax.rem(me_f, sharing) * groups + b * PER
        taps = taps_v[pl.ds(pl.multiple_of(first, PER), PER), :]
        for g in range(PER):
            band = pltpu.roll(
                jnp.broadcast_to(taps[g:g + 1], (LF, LANES)), 0, 1, stride=1, stride_axis=0)
            zero = jnp.zeros_like(band)
            toep_v[b, g * LF:(g + 1) * LF, :LANES] = jnp.where(above, band, zero).astype(BF16)
            toep_v[b, g * LF:(g + 1) * LF, LANES:] = jnp.where(above, zero, band).astype(BF16)

    def conv(b, p):
        lanes = lanes_of(b)
        at = 2 * LF * p
        prod = jnp.dot(toep_v[b], windows(p, lanes), preferred_element_type=F32)
        owner = lax.div(lax.broadcasted_iota(jnp.int32, (LF, 2 * LANES), 1), GS)
        owner = lax.rem(owner, PER)
        out = prod[:LF]
        for g in range(1, PER):
            out = jnp.where(owner == g, prod[g * LF:(g + 1) * LF], out)
        skip = skip_ref[pl.ds(b, 1), :]
        for half in range(2):
            here = slice(at + half * LF, at + (half + 1) * LF)
            direct = skip * sg_v[here, lanes].astype(F32)
            ig_ref[here, lanes] = (
                out[:, half * LANES:(half + 1) * LANES] + direct).astype(BF16)

    correlate_own(blocks - 2)
    correlate_own(blocks - 1)
    if fused:
        @pl.when(me_f < fsdp_size - 1)
        def _():
            pl.semaphore_wait(row_sem, fsdp_size - 1 - me_f)

        send_taps(me_f + 1, fsdp_size)
    early_pairs = (blocks // 2 - 1) // 2 + 1
    lax.fori_loop(0, early_pairs, correlate_two, 0)
    if fused:
        @pl.when(me_s < seq_size - 1)
        def _():
            pl.semaphore_wait(late_sem, seq_size - 1 - me_s)

        greet(all_sem, row, me)
        greet(all_sem, me + 1, row_end)
        send_bias(me_s + 1, seq_size)
    lax.fori_loop(early_pairs, blocks // 2 - 1, correlate_two, 0)
    halo_arrival(blocks // 2 - 1)
    here = pl.ds(groups - 2 * PER, 2 * PER)
    part_v[here, :] = part_v[here, :] + jnp.concatenate(
        [correlate_next(blocks - 2), correlate_next(blocks - 1)], axis=0)

    if fused:
        half_taps = width // 2
        pack_v[:groups, :] = part_v[...]
        pack_v[groups:, :] = pltpu.roll(part_v[...], LANES - half_taps, 1)
        turned = pack_v[...].T.astype(BF16)
        for f in range(fsdp_size):
            send_v[f] = turned[f * width:f * width + half_taps]
        recv_v[me] = send_v[me_f]
        pl.semaphore_wait(all_sem, fsdp_size - 1)

        def send_terms(other, c):
            o_s, o_f = lax.div(other, fsdp_size), lax.rem(other, fsdp_size)
            pltpu.make_async_remote_copy(
                src_ref=send_v.at[o_f], dst_ref=recv_v.at[me],
                send_sem=term_send, recv_sem=term_recv,
                device_id=(o_s, o_f), device_id_type=MESH).start()
            return c

        lax.fori_loop(0, me, send_terms, 0)
        lax.fori_loop(me + 1, total, send_terms, 0)

    loads[5].wait()
    loads[6].wait()
    for d in range(1, fsdp_size):
        tap_arrival(d).wait_recv()
    taps_v[...] = taps_r[...].T

    def build_conv(b, c):
        build(b)
        for p in range(pairs):
            conv(b, p)
        return c

    lax.fori_loop(0, blocks, build_conv, 0, unroll=2)

    for d in range(1, fsdp_size):
        tap_copy(lax.rem(me_f + d, fsdp_size)).wait_send()

    @pl.when(me_s > 0)
    def _():
        halo_copy(me_s - 1, 0, blocks).wait_send()

    if fused:
        def every(ref, slots, send_sem, recv_sem):
            span = ref.at[pl.ds(0, slots)]
            return pltpu.make_async_remote_copy(
                src_ref=span, dst_ref=span, send_sem=send_sem, recv_sem=recv_sem,
                device_id=(lax.rem(me_s + 1, seq_size), me_f), device_id_type=MESH)

        biases = every(bias_r, seq_size - 1, bias_send, bias_recv)
        biases.wait_send()
        biases.wait_recv()
        bias_r[me_s] = bias_v[...]
        bias_total = bias_r[0]
        for k in range(1, seq_size):
            bias_total = bias_total + bias_r[k]
        bias_ref[...] = bias_total
        terms = every(recv_v, total - 1, term_send, term_recv)
        terms.wait_send()
        terms.wait_recv()
        lane = lax.broadcasted_iota(jnp.int32, (half_taps, LANES), 1)
        sums = []
        for f in range(fsdp_size):
            piece = recv_v[f].astype(F32)
            for k in range(1, seq_size):
                piece = piece + recv_v[k * fsdp_size + f].astype(F32)
            sums.append(piece)
        for f in range(0, fsdp_size, 2):
            pair = pl.ds(f * groups, 2 * groups)
            fg_ref[:half_taps, pair] = jnp.where(
                lane < groups, sums[f], pltpu.roll(sums[f + 1], groups, 1))
            fg_ref[half_taps:, pair] = jnp.where(
                lane < groups, pltpu.roll(sums[f], groups, 1), sums[f + 1])
    else:
        fg_ref[...] = part_v[...]
        bias_ref[...] = bias_v[...]


def writer(*refs):
    count = len(refs) // 2
    sources, targets, sems = refs[:count], refs[count:2 * count], refs[2 * count]
    copies = [
        pltpu.make_async_copy(a, b, sems.at[i]) for i, (a, b) in enumerate(zip(sources, targets))]
    for copy in copies:
        copy.start()
    for copy in copies:
        copy.wait()


def write_out(*arrays):
    return pl.pallas_call(
        writer,
        out_shape=tuple(pltpu.HBM(a.shape, a.dtype) for a in arrays),
        in_specs=[pl.BlockSpec(memory_space=pltpu.VMEM)] * len(arrays),
        out_specs=(pl.BlockSpec(memory_space=pltpu.HBM),) * len(arrays),
        scratch_shapes=[pltpu.SemaphoreType.DMA((len(arrays),))],
    )(*(pltpu.with_memory_space_constraint(a, pltpu.VMEM) for a in arrays))


def on_device(seq_size, fsdp_size, conv_input, gate, out_grad, filters, skip_bias):
    rows, chans = conv_input.shape
    blocks = chans // LANES
    groups = chans // GS
    width = LF // fsdp_size
    fused = (
        seq_size <= 8 and fsdp_size % 2 == 0
        and 2 * groups == LANES)
    everyone = seq_size * fsdp_size if fused else 1
    fg_shape = (width, fsdp_size * groups) if fused else (groups, LF)
    half_taps = width // 2
    hbm_spec = pl.BlockSpec(memory_space=pltpu.HBM)
    vmem_spec = pl.BlockSpec(memory_space=pltpu.VMEM)
    dma = pltpu.SemaphoreType.DMA
    input_grad, filter_part, bias_part = pl.pallas_call(
        functools.partial(kernel, seq_size, fsdp_size, fused),
        out_shape=(
            jax.ShapeDtypeStruct((rows, chans), BF16),
            jax.ShapeDtypeStruct(fg_shape, F32),
            jax.ShapeDtypeStruct((blocks, LANES), F32),
        ),
        in_specs=[hbm_spec] * 5,
        out_specs=(vmem_spec, vmem_spec, vmem_spec),
        scratch_shapes=[
            pltpu.VMEM((blocks, LANES), F32),
            pltpu.VMEM((rows, chans), BF16),
            pltpu.VMEM((rows, chans), BF16),
            pltpu.VMEM((rows, chans), BF16),
            pltpu.VMEM((rows + LF, chans), BF16),
            pltpu.VMEM((blocks, PER * LF, 2 * LANES), BF16),
            pltpu.VMEM((LF, LANES), F32),
            pltpu.VMEM((LANES, LF), F32),
            pltpu.VMEM((groups, LANES), F32),
            pltpu.VMEM((blocks, LANES), F32),
            pltpu.VMEM((2 * groups, LANES), F32),
            pltpu.VMEM((fsdp_size, half_taps, LANES), BF16),
            pltpu.VMEM((everyone, half_taps, LANES), BF16),
            pltpu.VMEM((everyone // fsdp_size if fused else 1, blocks, LANES), F32),
            dma((7,)),
            dma,
            dma((blocks // 2,)),
            dma((fsdp_size,)),
            dma((fsdp_size,)),
            pltpu.SemaphoreType.REGULAR,
            pltpu.SemaphoreType.REGULAR,
            pltpu.SemaphoreType.REGULAR,
            dma,
            dma,
            dma,
            dma,
        ],
        compiler_params=pltpu.CompilerParams(
            collective_id=0, has_side_effects=True, vmem_limit_bytes=VMEM_GRANT),
    )(*(pltpu.with_memory_space_constraint(a, pltpu.HBM) for a in (
        conv_input, gate, out_grad, filters.T, skip_bias.reshape(blocks, LANES))))
    if fused:
        input_grad, filter_part, bias_part = write_out(input_grad, filter_part, bias_part)
        return input_grad, filter_part.T, bias_part.reshape(chans)
    spread = lax.all_to_all(
        filter_part, "fsdp", split_axis=1, concat_axis=0, tiled=True)
    filter_grad, bias_grad = lax.psum((spread, bias_part.reshape(chans)), "seq")
    return input_grad, filter_grad, bias_grad


def solution(mesh):
    placed = (P("seq", "fsdp"), P("seq", "fsdp"), P("seq", "fsdp"), P(None, "fsdp"), P("fsdp"))
    return jax.shard_map(
        functools.partial(on_device, mesh.shape["seq"], mesh.shape["fsdp"]),
        mesh=mesh,
        in_specs=placed,
        out_specs=(P("seq", "fsdp"), P(None, "fsdp"), P("fsdp")),
        check_vma=False,
    )
```

```python
import functools

import jax
import jax.numpy as jnp
from jax import lax
from jax.experimental import pallas as pl
from jax.experimental.pallas import tpu as pltpu
from jax.sharding import PartitionSpec as P

GS = 16
VMEM_GRANT = 105 << 19
LF = 128
LANES = 128
PER = LANES // GS
MESH = pl.DeviceIdType.MESH
F32 = jnp.float32
BF16 = jnp.bfloat16


def kernel(
    seq_size, fsdp_size, fused,
    x_hbm, gate_hbm, og_hbm, filt_hbm, skip_hbm,
    ig_ref, fg_ref, bias_ref,
    skip_ref, x_v, gate_v, og_v, sg_v, toep_v, filt_v, filt_b, taps_r, taps_v, part_v, bias_v,
    pack_v, send_v, recv_v, bias_r,
    load_sem, halo_send, halo_recv, tap_send, tap_recv, row_sem, late_sem, all_sem, term_send, term_recv, bias_send, bias_recv,
):
    rows, chans = x_v.shape
    blocks = chans // LANES
    pairs = rows // (2 * LF)
    groups = chans // GS
    me_s = lax.axis_index("seq")
    me_f = lax.axis_index("fsdp")

    width = LF // fsdp_size
    sharing = LANES // groups

    def tap_lanes(owner):
        return pl.ds(pl.multiple_of(lax.div(owner, sharing) * LANES, LANES), LANES)

    def tap_rows(source):
        return pl.ds(pl.multiple_of(source * width, width), width)

    rim = pl.ds(0, LF)
    rest = pl.ds(LF, rows - LF)
    loads = [
        pltpu.make_async_copy(og_hbm.at[rim], og_v.at[rim], load_sem.at[0]),
        pltpu.make_async_copy(gate_hbm.at[rim], gate_v.at[rim], load_sem.at[1]),
        pltpu.make_async_copy(og_hbm.at[rest], og_v.at[rest], load_sem.at[2]),
        pltpu.make_async_copy(gate_hbm.at[rest], gate_v.at[rest], load_sem.at[3]),
        pltpu.make_async_copy(x_hbm, x_v, load_sem.at[4]),
        pltpu.make_async_copy(filt_hbm, filt_v, load_sem.at[5]),
        pltpu.make_async_copy(skip_hbm, skip_ref, load_sem.at[6]),
    ]
    barrier = pltpu.get_barrier_semaphore()
    def greet(semaphore, first, end):
        def step(other, c):
            o_s, o_f = lax.div(other, fsdp_size), lax.rem(other, fsdp_size)
            pl.semaphore_signal(
                semaphore, inc=1, device_id=(o_s, o_f), device_id_type=MESH)
            return c

        lax.fori_loop(first, end, step, 0)

    if fused:
        me = me_s * fsdp_size + me_f
        total = seq_size * fsdp_size
        row = me_s * fsdp_size
        row_end = row + fsdp_size

        def greet_column(semaphore, first, end):
            def step(o_s, c):
                pl.semaphore_signal(semaphore, inc=1, device_id=(o_s, me_f), device_id_type=MESH)
                return c

            lax.fori_loop(first, end, step, 0)

        greet_column(barrier, me_s + 1, seq_size)
        greet(barrier, me + 1, row_end)
    else:
        for d in range(1, fsdp_size):
            pl.semaphore_signal(
                barrier, inc=1, device_id=(me_s, lax.rem(me_f + d, fsdp_size)),
                device_id_type=MESH)

        @pl.when(me_s > 0)
        def _():
            pl.semaphore_signal(
                barrier, inc=1, device_id=(me_s - 1, me_f), device_id_type=MESH)

        @pl.when(me_s < seq_size - 1)
        def _():
            pl.semaphore_signal(
                barrier, inc=1, device_id=(me_s + 1, me_f), device_id_type=MESH)

    for load in loads:
        load.start()
    loads[0].wait()
    loads[1].wait()
    sg_v[rim, :] = (og_v[rim, :].astype(F32) * gate_v[rim, :].astype(F32)).astype(BF16)

    if fused:
        @pl.when(me_s + me_f > 0)
        def _():
            pl.semaphore_wait(barrier, me_s + me_f)
    else:
        pl.semaphore_wait(barrier, fsdp_size - 1)

        @pl.when(me_s > 0)
        def _():
            pl.semaphore_wait(barrier, 1)

        @pl.when(me_s < seq_size - 1)
        def _():
            pl.semaphore_wait(barrier, 1)

    def lanes_of(b):
        return pl.ds(pl.multiple_of(b * LANES, LANES), LANES)

    def halo_copy(target, first, end):
        lanes = pl.ds(first * LANES, (end - first) * LANES)
        return pltpu.make_async_remote_copy(
            src_ref=sg_v.at[rim, lanes], dst_ref=sg_v.at[pl.ds(rows, LF), lanes],
            send_sem=halo_send, recv_sem=halo_recv.at[first // 2],
            device_id=(target, me_f), device_id_type=MESH)

    @pl.when(me_s > 0)
    def _():
        for b in range(0, blocks, 2):
            halo_copy(me_s - 1, b, b + 2).start()

    def tap_copy(other):
        return pltpu.make_async_remote_copy(
            src_ref=filt_b.at[:, tap_lanes(other)],
            dst_ref=taps_r.at[tap_rows(me_f)],
            send_sem=tap_send.at[other], recv_sem=tap_recv.at[me_f],
            device_id=(me_s, other), device_id_type=MESH)

    def tap_arrival(d):
        other = lax.rem(me_f + d, fsdp_size)
        return pltpu.make_async_remote_copy(
            src_ref=filt_b.at[:, tap_lanes(other)],
            dst_ref=taps_r.at[tap_rows(other)],
            send_sem=tap_send.at[other], recv_sem=tap_recv.at[other],
            device_id=(me_s, other), device_id_type=MESH)

    loads[5].wait()
    filt_b[...] = filt_v[...].astype(BF16)
    taps_r[tap_rows(me_f), :] = filt_b[:, tap_lanes(me_f)]

    def send_taps(first, end):
        def step(other, c):
            tap_copy(other).start()
            return c

        lax.fori_loop(first, end, step, 0)

    if fused:
        greet(row_sem, row, me)
        greet_column(late_sem, 0, me_s)
    else:
        send_taps(me_f + 1, fsdp_size)
    send_taps(0, me_f)

    @pl.when(me_s == seq_size - 1)
    def _():
        sg_v[pl.ds(rows, LF), :] = jnp.zeros((LF, chans), BF16)

    for load in loads[2:5]:
        load.wait()

    def scale(b, c):
        lanes = lanes_of(b)
        new = (og_v[rest, lanes].astype(F32) * gate_v[rest, lanes].astype(F32)).astype(BF16)
        sg_v[rest, lanes] = new
        terms = jnp.sum(new.astype(F32) * x_v[rest, lanes].astype(F32), axis=0, keepdims=True)
        terms = terms + jnp.sum(
            sg_v[rim, lanes].astype(F32) * x_v[rim, lanes].astype(F32), axis=0, keepdims=True)
        bias_v[pl.ds(b, 1), :] = terms
        return c

    lax.fori_loop(0, blocks, scale, 0, unroll=2)

    if fused:
        def bias_copy(o_s):
            return pltpu.make_async_remote_copy(
                src_ref=bias_v, dst_ref=bias_r.at[me_s], send_sem=bias_send, recv_sem=bias_recv,
                device_id=(o_s, me_f), device_id_type=MESH)

        def send_bias(first, end):
            def step(o_s, c):
                bias_copy(o_s).start()
                return c

            lax.fori_loop(first, end, step, 0)

        send_bias(0, me_s)

    row_at = lax.broadcasted_iota(jnp.int32, (LF, LANES), 0)
    lane_at = lax.broadcasted_iota(jnp.int32, (LF, LANES), 1)
    above = lane_at >= row_at

    def windows(p, lanes):
        at = 2 * LF * p
        return jnp.concatenate(
            [sg_v[at:at + 2 * LF, lanes], sg_v[at + LF:at + 3 * LF, lanes]], axis=1)

    def split_groups(both):
        lane = lax.broadcasted_iota(jnp.int32, both.shape, 1)
        owner = lax.rem(lax.div(lane, GS), PER)
        return jnp.concatenate(
            [both * (owner == g).astype(F32).astype(BF16) for g in range(PER)], axis=0)

    def products(left, right):
        return lax.dot_general(
            split_groups(left), right, (((1,), (1,)), ((), ())), preferred_element_type=F32)

    def fold(wrapped):
        parts = [wrapped[:8]] + [
            pltpu.roll(wrapped[8 * k:8 * k + 8], LANES - 8 * k, 1) for k in range(1, LF // 8)]
        while len(parts) > 1:
            parts = [one + two for one, two in zip(parts[::2], parts[1::2])]
        return parts[0]

    sub = lax.broadcasted_iota(jnp.int32, (8, LANES), 0)

    def diagonals(wholes):
        for bit in (2, 1, 0):
            step = 1 << bit
            odd = lax.rem(lax.div(sub, step), 2) == 1
            wholes = [
                jnp.where(odd, pltpu.roll(wholes[i + step], step, 0), wholes[i])
                + pltpu.roll(
                    jnp.where(odd, wholes[i + step], pltpu.roll(wholes[i], 8 - step, 0)),
                    LANES - step, 1)
                for i in range(step)]
        return wholes[0]

    def tiles(ref, lanes, span, count):
        return jnp.concatenate([ref[at:at + span, lanes] for at in range(0, count * LF, LF)], axis=1)

    def correlate(b):
        lanes = lanes_of(b)
        prod = products(
            tiles(x_v, lanes, LF, rows // LF), tiles(sg_v, lanes, 2 * LF, rows // LF))
        wholes = []
        for g in range(PER):
            one = prod[g * LF:(g + 1) * LF]
            wholes.append(fold(jnp.where(above, one[:, :LANES], one[:, LANES:])))
        part_v[pl.ds(pl.multiple_of(b * PER, PER), PER), :] = diagonals(wholes)

    def correlate_own(b):
        lanes = lanes_of(b)
        last = jnp.concatenate(
            [sg_v[rows - LF:rows, lanes], jnp.zeros((LF, LANES), BF16)], axis=0)
        prod = products(
            tiles(x_v, lanes, LF, rows // LF),
            jnp.concatenate([tiles(sg_v, lanes, 2 * LF, rows // LF - 1), last], axis=1))
        wholes = []
        for g in range(PER):
            one = prod[g * LF:(g + 1) * LF]
            wholes.append(fold(jnp.where(above, one[:, :LANES], one[:, LANES:])))
        part_v[b * PER:(b + 1) * PER, :] = diagonals(wholes)

    def correlate_next(b):
        lanes = lanes_of(b)
        prod = products(x_v[rows - LF:rows, lanes], sg_v[rows:rows + LF, lanes])
        wholes = []
        for g in range(PER):
            one = prod[g * LF:(g + 1) * LF]
            wholes.append(fold(jnp.where(above, jnp.zeros_like(one), one)))
        return diagonals(wholes)

    def halo_arrival(i):
        @pl.when(me_s < seq_size - 1)
        def _():
            lanes = pl.ds(pl.multiple_of(i * 2 * LANES, 2 * LANES), 2 * LANES)
            pltpu.make_async_remote_copy(
                src_ref=sg_v.at[rim, lanes], dst_ref=sg_v.at[pl.ds(rows, LF), lanes],
                send_sem=halo_send, recv_sem=halo_recv.at[i],
                device_id=(me_s + 1, me_f), device_id_type=MESH).wait_recv()

    def correlate_two(i, c):
        halo_arrival(i)
        correlate(2 * i)
        correlate(2 * i + 1)
        return c

    def build(b):
        first = lax.rem(me_f, sharing) * groups + b * PER
        taps = taps_v[pl.ds(pl.multiple_of(first, PER), PER), :]
        for g in range(PER):
            band = pltpu.roll(
                jnp.broadcast_to(taps[g:g + 1], (LF, LANES)), 0, 1, stride=1, stride_axis=0)
            zero = jnp.zeros_like(band)
            toep_v[b, g * LF:(g + 1) * LF, :LANES] = jnp.where(above, band, zero).astype(BF16)
            toep_v[b, g * LF:(g + 1) * LF, LANES:] = jnp.where(above, zero, band).astype(BF16)

    def conv(b, p):
        lanes = lanes_of(b)
        at = 2 * LF * p
        prod = jnp.dot(toep_v[b], windows(p, lanes), preferred_element_type=F32)
        owner = lax.div(lax.broadcasted_iota(jnp.int32, (LF, 2 * LANES), 1), GS)
        owner = lax.rem(owner, PER)
        out = prod[:LF]
        for g in range(1, PER):
            out = jnp.where(owner == g, prod[g * LF:(g + 1) * LF], out)
        skip = skip_ref[pl.ds(b, 1), :]
        for half in range(2):
            here = slice(at + half * LF, at + (half + 1) * LF)
            direct = skip * sg_v[here, lanes].astype(F32)
            ig_ref[here, lanes] = (
                out[:, half * LANES:(half + 1) * LANES] + direct).astype(BF16)

    correlate_own(blocks - 2)
    correlate_own(blocks - 1)
    if fused:
        @pl.when(me_f < fsdp_size - 1)
        def _():
            pl.semaphore_wait(row_sem, fsdp_size - 1 - me_f)

        send_taps(me_f + 1, fsdp_size)
    early_pairs = (blocks // 2 - 1) // 2 + 1
    lax.fori_loop(0, early_pairs, correlate_two, 0)
    if fused:
        @pl.when(me_s < seq_size - 1)
        def _():
            pl.semaphore_wait(late_sem, seq_size - 1 - me_s)

        greet(all_sem, row, me)
        greet(all_sem, me + 1, row_end)
        send_bias(me_s + 1, seq_size)
    lax.fori_loop(early_pairs, blocks // 2 - 1, correlate_two, 0)
    halo_arrival(blocks // 2 - 1)
    here = pl.ds(groups - 2 * PER, 2 * PER)
    part_v[here, :] = part_v[here, :] + jnp.concatenate(
        [correlate_next(blocks - 2), correlate_next(blocks - 1)], axis=0)

    if fused:
        half_taps = width // 2
        pack_v[:groups, :] = part_v[...]
        pack_v[groups:, :] = pltpu.roll(part_v[...], LANES - half_taps, 1)
        turned = pack_v[...].T.astype(BF16)
        for f in range(fsdp_size):
            send_v[f] = turned[f * width:f * width + half_taps]
        recv_v[me] = send_v[me_f]
        pl.semaphore_wait(all_sem, fsdp_size - 1)

        def send_terms(other, c):
            o_s, o_f = lax.div(other, fsdp_size), lax.rem(other, fsdp_size)
            pltpu.make_async_remote_copy(
                src_ref=send_v.at[o_f], dst_ref=recv_v.at[me],
                send_sem=term_send, recv_sem=term_recv,
                device_id=(o_s, o_f), device_id_type=MESH).start()
            return c

        def send_place(o_s, c):
            for d_f in range(fsdp_size):
                send_terms(o_s * fsdp_size + lax.rem(me_f + d_f, fsdp_size), c)
            return c

        lax.fori_loop(0, me_s, send_place, 0)
        lax.fori_loop(0, seq_size - 1 - me_s, lambda i, c: send_place(seq_size - 1 - i, c), 0)
        for d_f in range(1, fsdp_size):
            send_terms(row + lax.rem(me_f + d_f, fsdp_size), 0)

    loads[6].wait()
    for d in range(1, fsdp_size):
        tap_arrival(d).wait_recv()
    taps_v[...] = taps_r[...].astype(F32).T

    def build_conv(b, c):
        build(b)
        for p in range(pairs):
            conv(b, p)
        return c

    lax.fori_loop(0, blocks, build_conv, 0, unroll=2)

    for d in range(1, fsdp_size):
        tap_copy(lax.rem(me_f + d, fsdp_size)).wait_send()

    @pl.when(me_s > 0)
    def _():
        halo_copy(me_s - 1, 0, blocks).wait_send()

    if fused:
        def every(ref, slots, send_sem, recv_sem):
            span = ref.at[pl.ds(0, slots)]
            return pltpu.make_async_remote_copy(
                src_ref=span, dst_ref=span, send_sem=send_sem, recv_sem=recv_sem,
                device_id=(lax.rem(me_s + 1, seq_size), me_f), device_id_type=MESH)

        biases = every(bias_r, seq_size - 1, bias_send, bias_recv)
        biases.wait_send()
        biases.wait_recv()
        bias_r[me_s] = bias_v[...]
        bias_total = bias_r[0]
        for k in range(1, seq_size):
            bias_total = bias_total + bias_r[k]
        bias_ref[...] = bias_total
        terms = every(recv_v, total - 1, term_send, term_recv)
        terms.wait_send()
        terms.wait_recv()
        lane = lax.broadcasted_iota(jnp.int32, (half_taps, LANES), 1)
        sums = []
        for f in range(fsdp_size):
            piece = recv_v[f].astype(F32)
            for k in range(1, seq_size):
                piece = piece + recv_v[k * fsdp_size + f].astype(F32)
            sums.append(piece)
        for f in range(0, fsdp_size, 2):
            pair = pl.ds(f * groups, 2 * groups)
            fg_ref[:half_taps, pair] = jnp.where(
                lane < groups, sums[f], pltpu.roll(sums[f + 1], groups, 1))
            fg_ref[half_taps:, pair] = jnp.where(
                lane < groups, pltpu.roll(sums[f], groups, 1), sums[f + 1])
    else:
        fg_ref[...] = part_v[...]
        bias_ref[...] = bias_v[...]


def writer(*refs):
    count = len(refs) // 2
    sources, targets, sems = refs[:count], refs[count:2 * count], refs[2 * count]
    copies = [
        pltpu.make_async_copy(a, b, sems.at[i]) for i, (a, b) in enumerate(zip(sources, targets))]
    for copy in copies:
        copy.start()
    for copy in copies:
        copy.wait()


def write_out(*arrays):
    return pl.pallas_call(
        writer,
        out_shape=tuple(pltpu.HBM(a.shape, a.dtype) for a in arrays),
        in_specs=[pl.BlockSpec(memory_space=pltpu.VMEM)] * len(arrays),
        out_specs=(pl.BlockSpec(memory_space=pltpu.HBM),) * len(arrays),
        scratch_shapes=[pltpu.SemaphoreType.DMA((len(arrays),))],
    )(*(pltpu.with_memory_space_constraint(a, pltpu.VMEM) for a in arrays))


def on_device(seq_size, fsdp_size, conv_input, gate, out_grad, filters, skip_bias):
    rows, chans = conv_input.shape
    blocks = chans // LANES
    groups = chans // GS
    width = LF // fsdp_size
    fused = (
        seq_size <= 8 and fsdp_size % 2 == 0
        and 2 * groups == LANES)
    everyone = seq_size * fsdp_size if fused else 1
    fg_shape = (width, fsdp_size * groups) if fused else (groups, LF)
    half_taps = width // 2
    hbm_spec = pl.BlockSpec(memory_space=pltpu.HBM)
    vmem_spec = pl.BlockSpec(memory_space=pltpu.VMEM)
    dma = pltpu.SemaphoreType.DMA
    input_grad, filter_part, bias_part = pl.pallas_call(
        functools.partial(kernel, seq_size, fsdp_size, fused),
        out_shape=(
            jax.ShapeDtypeStruct((rows, chans), BF16),
            jax.ShapeDtypeStruct(fg_shape, F32),
            jax.ShapeDtypeStruct((blocks, LANES), F32),
        ),
        in_specs=[hbm_spec] * 5,
        out_specs=(vmem_spec, vmem_spec, vmem_spec),
        scratch_shapes=[
            pltpu.VMEM((blocks, LANES), F32),
            pltpu.VMEM((rows, chans), BF16),
            pltpu.VMEM((rows, chans), BF16),
            pltpu.VMEM((rows, chans), BF16),
            pltpu.VMEM((rows + LF, chans), BF16),
            pltpu.VMEM((blocks, PER * LF, 2 * LANES), BF16),
            pltpu.VMEM((width, fsdp_size * groups), F32),
            pltpu.VMEM((width, fsdp_size * groups), BF16),
            pltpu.VMEM((LF, LANES), BF16),
            pltpu.VMEM((LANES, LF), F32),
            pltpu.VMEM((groups, LANES), F32),
            pltpu.VMEM((blocks, LANES), F32),
            pltpu.VMEM((2 * groups, LANES), F32),
            pltpu.VMEM((fsdp_size, half_taps, LANES), BF16),
            pltpu.VMEM((everyone, half_taps, LANES), BF16),
            pltpu.VMEM((everyone // fsdp_size if fused else 1, blocks, LANES), F32),
            dma((7,)),
            dma,
            dma((blocks // 2,)),
            dma((fsdp_size,)),
            dma((fsdp_size,)),
            pltpu.SemaphoreType.REGULAR,
            pltpu.SemaphoreType.REGULAR,
            pltpu.SemaphoreType.REGULAR,
            dma,
            dma,
            dma,
            dma,
        ],
        compiler_params=pltpu.CompilerParams(
            collective_id=0, has_side_effects=True, vmem_limit_bytes=VMEM_GRANT),
    )(*(pltpu.with_memory_space_constraint(a, pltpu.HBM) for a in (
        conv_input, gate, out_grad, filters.T, skip_bias.reshape(blocks, LANES))))
    if fused:
        input_grad, filter_part, bias_part = write_out(input_grad, filter_part, bias_part)
        return input_grad, filter_part.T, bias_part.reshape(chans)
    spread = lax.all_to_all(
        filter_part, "fsdp", split_axis=1, concat_axis=0, tiled=True)
    filter_grad, bias_grad = lax.psum((spread, bias_part.reshape(chans)), "seq")
    return input_grad, filter_grad, bias_grad


def solution(mesh):
    placed = (P("seq", "fsdp"), P("seq", "fsdp"), P("seq", "fsdp"), P(None, "fsdp"), P("fsdp"))
    return jax.shard_map(
        functools.partial(on_device, mesh.shape["seq"], mesh.shape["fsdp"]),
        mesh=mesh,
        in_specs=placed,
        out_specs=(P("seq", "fsdp"), P(None, "fsdp"), P("fsdp")),
        check_vma=False,
    )
```

```python
import functools

import jax
import jax.numpy as jnp
from jax import lax
from jax.experimental import pallas as pl
from jax.experimental.pallas import tpu as pltpu
from jax.sharding import PartitionSpec as P

GS = 16
VMEM_GRANT = 105 << 19
LF = 128
LANES = 128
PER = LANES // GS
MESH = pl.DeviceIdType.MESH
F32 = jnp.float32
BF16 = jnp.bfloat16


def kernel(
    seq_size, fsdp_size, fused,
    x_hbm, gate_hbm, og_hbm, filt_hbm, skip_hbm,
    ig_ref, fg_ref, bias_ref,
    skip_ref, x_v, gate_v, og_v, sg_v, toep_v, filt_v, filt_b, taps_r, taps_v, part_v, bias_v,
    pack_v, send_v, recv_v, bias_r,
    load_sem, halo_send, halo_recv, tap_send, tap_recv, row_sem, late_sem, all_sem, term_send, term_recv, bias_send, bias_recv,
):
    rows, chans = x_v.shape
    blocks = chans // LANES
    pairs = rows // (2 * LF)
    groups = chans // GS
    me_s = lax.axis_index("seq")
    me_f = lax.axis_index("fsdp")

    width = LF // fsdp_size
    sharing = LANES // groups

    def tap_lanes(owner):
        return pl.ds(pl.multiple_of(lax.div(owner, sharing) * LANES, LANES), LANES)

    def tap_rows(source):
        return pl.ds(pl.multiple_of(source * width, width), width)

    rim = pl.ds(0, LF)
    rest = pl.ds(LF, rows - LF)
    loads = [
        pltpu.make_async_copy(og_hbm.at[rim], og_v.at[rim], load_sem.at[0]),
        pltpu.make_async_copy(gate_hbm.at[rim], gate_v.at[rim], load_sem.at[1]),
        pltpu.make_async_copy(og_hbm.at[rest], og_v.at[rest], load_sem.at[2]),
        pltpu.make_async_copy(gate_hbm.at[rest], gate_v.at[rest], load_sem.at[3]),
        pltpu.make_async_copy(x_hbm, x_v, load_sem.at[4]),
        pltpu.make_async_copy(filt_hbm, filt_v, load_sem.at[5]),
        pltpu.make_async_copy(skip_hbm, skip_ref, load_sem.at[6]),
    ]
    barrier = pltpu.get_barrier_semaphore()
    def greet(semaphore, first, end):
        def step(other, c):
            o_s, o_f = lax.div(other, fsdp_size), lax.rem(other, fsdp_size)
            pl.semaphore_signal(
                semaphore, inc=1, device_id=(o_s, o_f), device_id_type=MESH)
            return c

        lax.fori_loop(first, end, step, 0)

    if fused:
        me = me_s * fsdp_size + me_f
        total = seq_size * fsdp_size
        row = me_s * fsdp_size
        row_end = row + fsdp_size

        def greet_column(semaphore, first, end):
            def step(o_s, c):
                pl.semaphore_signal(semaphore, inc=1, device_id=(o_s, me_f), device_id_type=MESH)
                return c

            lax.fori_loop(first, end, step, 0)

        greet_column(barrier, me_s + 1, seq_size)
        greet(barrier, me + 1, row_end)
    else:
        for d in range(1, fsdp_size):
            pl.semaphore_signal(
                barrier, inc=1, device_id=(me_s, lax.rem(me_f + d, fsdp_size)),
                device_id_type=MESH)

        @pl.when(me_s > 0)
        def _():
            pl.semaphore_signal(
                barrier, inc=1, device_id=(me_s - 1, me_f), device_id_type=MESH)

        @pl.when(me_s < seq_size - 1)
        def _():
            pl.semaphore_signal(
                barrier, inc=1, device_id=(me_s + 1, me_f), device_id_type=MESH)

    for load in loads:
        load.start()
    loads[0].wait()
    loads[1].wait()
    sg_v[rim, :] = (og_v[rim, :].astype(F32) * gate_v[rim, :].astype(F32)).astype(BF16)

    if fused:
        @pl.when(me_s + me_f > 0)
        def _():
            pl.semaphore_wait(barrier, me_s + me_f)
    else:
        pl.semaphore_wait(barrier, fsdp_size - 1)

        @pl.when(me_s > 0)
        def _():
            pl.semaphore_wait(barrier, 1)

        @pl.when(me_s < seq_size - 1)
        def _():
            pl.semaphore_wait(barrier, 1)

    def lanes_of(b):
        return pl.ds(pl.multiple_of(b * LANES, LANES), LANES)

    def halo_copy(target, first, end):
        lanes = pl.ds(first * LANES, (end - first) * LANES)
        return pltpu.make_async_remote_copy(
            src_ref=sg_v.at[rim, lanes], dst_ref=sg_v.at[pl.ds(rows, LF), lanes],
            send_sem=halo_send, recv_sem=halo_recv.at[first // 2],
            device_id=(target, me_f), device_id_type=MESH)

    @pl.when(me_s > 0)
    def _():
        for b in range(0, blocks, 2):
            halo_copy(me_s - 1, b, b + 2).start()

    def tap_copy(other):
        return pltpu.make_async_remote_copy(
            src_ref=filt_b.at[:, tap_lanes(other)],
            dst_ref=taps_r.at[tap_rows(me_f)],
            send_sem=tap_send.at[other], recv_sem=tap_recv.at[me_f],
            device_id=(me_s, other), device_id_type=MESH)

    def tap_arrival(d):
        other = lax.rem(me_f + d, fsdp_size)
        return pltpu.make_async_remote_copy(
            src_ref=filt_b.at[:, tap_lanes(other)],
            dst_ref=taps_r.at[tap_rows(other)],
            send_sem=tap_send.at[other], recv_sem=tap_recv.at[other],
            device_id=(me_s, other), device_id_type=MESH)

    def send_taps(first, end):
        def step(other, c):
            tap_copy(other).start()
            return c

        lax.fori_loop(first, end, step, 0)

    if fused:
        greet_column(late_sem, 0, me_s)
        greet(row_sem, row, me)
    loads[5].wait()
    filt_b[...] = filt_v[...].astype(BF16)
    taps_r[tap_rows(me_f), :] = filt_b[:, tap_lanes(me_f)]

    if not fused:
        send_taps(me_f + 1, fsdp_size)
    send_taps(0, me_f)

    @pl.when(me_s == seq_size - 1)
    def _():
        sg_v[pl.ds(rows, LF), :] = jnp.zeros((LF, chans), BF16)

    for load in loads[2:5]:
        load.wait()

    def scale(b, c):
        lanes = lanes_of(b)
        new = (og_v[rest, lanes].astype(F32) * gate_v[rest, lanes].astype(F32)).astype(BF16)
        sg_v[rest, lanes] = new
        terms = jnp.sum(new.astype(F32) * x_v[rest, lanes].astype(F32), axis=0, keepdims=True)
        terms = terms + jnp.sum(
            sg_v[rim, lanes].astype(F32) * x_v[rim, lanes].astype(F32), axis=0, keepdims=True)
        bias_v[pl.ds(b, 1), :] = terms
        return c

    lax.fori_loop(0, blocks, scale, 0, unroll=2)

    if fused:
        def bias_copy(o_s):
            return pltpu.make_async_remote_copy(
                src_ref=bias_v, dst_ref=bias_r.at[me_s], send_sem=bias_send, recv_sem=bias_recv,
                device_id=(o_s, me_f), device_id_type=MESH)

        def send_bias(first, end):
            def step(o_s, c):
                bias_copy(o_s).start()
                return c

            lax.fori_loop(first, end, step, 0)

        send_bias(0, me_s)

    row_at = lax.broadcasted_iota(jnp.int32, (LF, LANES), 0)
    lane_at = lax.broadcasted_iota(jnp.int32, (LF, LANES), 1)
    above = lane_at >= row_at

    def windows(p, lanes):
        at = 2 * LF * p
        return jnp.concatenate(
            [sg_v[at:at + 2 * LF, lanes], sg_v[at + LF:at + 3 * LF, lanes]], axis=1)

    def split_groups(both):
        lane = lax.broadcasted_iota(jnp.int32, both.shape, 1)
        owner = lax.rem(lax.div(lane, GS), PER)
        return jnp.concatenate(
            [both * (owner == g).astype(F32).astype(BF16) for g in range(PER)], axis=0)

    def products(left, right):
        return lax.dot_general(
            split_groups(left), right, (((1,), (1,)), ((), ())), preferred_element_type=F32)

    def fold(wrapped):
        parts = [wrapped[:8]] + [
            pltpu.roll(wrapped[8 * k:8 * k + 8], LANES - 8 * k, 1) for k in range(1, LF // 8)]
        while len(parts) > 1:
            parts = [one + two for one, two in zip(parts[::2], parts[1::2])]
        return parts[0]

    sub = lax.broadcasted_iota(jnp.int32, (8, LANES), 0)

    def diagonals(wholes):
        for bit in (2, 1, 0):
            step = 1 << bit
            odd = lax.rem(lax.div(sub, step), 2) == 1
            wholes = [
                jnp.where(odd, pltpu.roll(wholes[i + step], step, 0), wholes[i])
                + pltpu.roll(
                    jnp.where(odd, wholes[i + step], pltpu.roll(wholes[i], 8 - step, 0)),
                    LANES - step, 1)
                for i in range(step)]
        return wholes[0]

    def tiles(ref, lanes, span, count):
        return jnp.concatenate([ref[at:at + span, lanes] for at in range(0, count * LF, LF)], axis=1)

    def correlate(b):
        lanes = lanes_of(b)
        prod = products(
            tiles(x_v, lanes, LF, rows // LF), tiles(sg_v, lanes, 2 * LF, rows // LF))
        wholes = []
        for g in range(PER):
            one = prod[g * LF:(g + 1) * LF]
            wholes.append(fold(jnp.where(above, one[:, :LANES], one[:, LANES:])))
        part_v[pl.ds(pl.multiple_of(b * PER, PER), PER), :] = diagonals(wholes)

    def correlate_own(b):
        lanes = lanes_of(b)
        last = jnp.concatenate(
            [sg_v[rows - LF:rows, lanes], jnp.zeros((LF, LANES), BF16)], axis=0)
        prod = products(
            tiles(x_v, lanes, LF, rows // LF),
            jnp.concatenate([tiles(sg_v, lanes, 2 * LF, rows // LF - 1), last], axis=1))
        wholes = []
        for g in range(PER):
            one = prod[g * LF:(g + 1) * LF]
            wholes.append(fold(jnp.where(above, one[:, :LANES], one[:, LANES:])))
        part_v[b * PER:(b + 1) * PER, :] = diagonals(wholes)

    def correlate_next(b):
        lanes = lanes_of(b)
        prod = products(x_v[rows - LF:rows, lanes], sg_v[rows:rows + LF, lanes])
        wholes = []
        for g in range(PER):
            one = prod[g * LF:(g + 1) * LF]
            wholes.append(fold(jnp.where(above, jnp.zeros_like(one), one)))
        return diagonals(wholes)

    def halo_arrival(i):
        @pl.when(me_s < seq_size - 1)
        def _():
            lanes = pl.ds(pl.multiple_of(i * 2 * LANES, 2 * LANES), 2 * LANES)
            pltpu.make_async_remote_copy(
                src_ref=sg_v.at[rim, lanes], dst_ref=sg_v.at[pl.ds(rows, LF), lanes],
                send_sem=halo_send, recv_sem=halo_recv.at[i],
                device_id=(me_s + 1, me_f), device_id_type=MESH).wait_recv()

    def correlate_two(i, c):
        halo_arrival(i)
        correlate(2 * i)
        correlate(2 * i + 1)
        return c

    def build(b):
        first = lax.rem(me_f, sharing) * groups + b * PER
        taps = taps_v[pl.ds(pl.multiple_of(first, PER), PER), :]
        for g in range(PER):
            band = pltpu.roll(
                jnp.broadcast_to(taps[g:g + 1], (LF, LANES)), 0, 1, stride=1, stride_axis=0)
            zero = jnp.zeros_like(band)
            toep_v[b, g * LF:(g + 1) * LF, :LANES] = jnp.where(above, band, zero).astype(BF16)
            toep_v[b, g * LF:(g + 1) * LF, LANES:] = jnp.where(above, zero, band).astype(BF16)

    def conv(b, p):
        lanes = lanes_of(b)
        at = 2 * LF * p
        prod = jnp.dot(toep_v[b], windows(p, lanes), preferred_element_type=F32)
        owner = lax.div(lax.broadcasted_iota(jnp.int32, (LF, 2 * LANES), 1), GS)
        owner = lax.rem(owner, PER)
        out = prod[:LF]
        for g in range(1, PER):
            out = jnp.where(owner == g, prod[g * LF:(g + 1) * LF], out)
        skip = skip_ref[pl.ds(b, 1), :]
        for half in range(2):
            here = slice(at + half * LF, at + (half + 1) * LF)
            direct = skip * sg_v[here, lanes].astype(F32)
            ig_ref[here, lanes] = (
                out[:, half * LANES:(half + 1) * LANES] + direct).astype(BF16)

    correlate_own(blocks - 2)
    correlate_own(blocks - 1)
    early_pairs = (blocks // 2 - 1) // 2 + 1
    lax.fori_loop(0, early_pairs, correlate_two, 0)
    if fused:
        @pl.when(me_f < fsdp_size - 1)
        def _():
            pl.semaphore_wait(row_sem, fsdp_size - 1 - me_f)

        send_taps(me_f + 1, fsdp_size)

        @pl.when(me_s < seq_size - 1)
        def _():
            pl.semaphore_wait(late_sem, seq_size - 1 - me_s)

        greet(all_sem, row, me)
        greet(all_sem, me + 1, row_end)
        send_bias(me_s + 1, seq_size)
    lax.fori_loop(early_pairs, blocks // 2 - 1, correlate_two, 0)
    halo_arrival(blocks // 2 - 1)
    here = pl.ds(groups - 2 * PER, 2 * PER)
    part_v[here, :] = part_v[here, :] + jnp.concatenate(
        [correlate_next(blocks - 2), correlate_next(blocks - 1)], axis=0)

    if fused:
        half_taps = width // 2
        pack_v[:groups, :] = part_v[...]
        pack_v[groups:, :] = pltpu.roll(part_v[...], LANES - half_taps, 1)
        turned = pack_v[...].T.astype(BF16)
        for f in range(fsdp_size):
            send_v[f] = turned[f * width:f * width + half_taps]
        recv_v[me] = send_v[me_f]
        pl.semaphore_wait(all_sem, fsdp_size - 1)

        def send_terms(other, c):
            o_s, o_f = lax.div(other, fsdp_size), lax.rem(other, fsdp_size)
            pltpu.make_async_remote_copy(
                src_ref=send_v.at[o_f], dst_ref=recv_v.at[me],
                send_sem=term_send, recv_sem=term_recv,
                device_id=(o_s, o_f), device_id_type=MESH).start()
            return c

        def send_place(o_s, c):
            for d_f in range(fsdp_size):
                send_terms(o_s * fsdp_size + lax.rem(me_f + d_f, fsdp_size), c)
            return c

        lax.fori_loop(0, me_s, send_place, 0)
        lax.fori_loop(0, seq_size - 1 - me_s, lambda i, c: send_place(seq_size - 1 - i, c), 0)
        for d_f in range(1, fsdp_size):
            send_terms(row + lax.rem(me_f + d_f, fsdp_size), 0)

    loads[6].wait()
    for d in range(1, fsdp_size):
        tap_arrival(d).wait_recv()
    taps_v[...] = taps_r[...].astype(F32).T

    def build_conv(b, c):
        build(b)
        for p in range(pairs):
            conv(b, p)
        return c

    lax.fori_loop(0, blocks, build_conv, 0, unroll=2)

    for d in range(1, fsdp_size):
        tap_copy(lax.rem(me_f + d, fsdp_size)).wait_send()

    @pl.when(me_s > 0)
    def _():
        halo_copy(me_s - 1, 0, blocks).wait_send()

    if fused:
        def every(ref, slots, send_sem, recv_sem):
            span = ref.at[pl.ds(0, slots)]
            return pltpu.make_async_remote_copy(
                src_ref=span, dst_ref=span, send_sem=send_sem, recv_sem=recv_sem,
                device_id=(lax.rem(me_s + 1, seq_size), me_f), device_id_type=MESH)

        biases = every(bias_r, seq_size - 1, bias_send, bias_recv)
        biases.wait_send()
        biases.wait_recv()
        bias_r[me_s] = bias_v[...]
        bias_total = bias_r[0]
        for k in range(1, seq_size):
            bias_total = bias_total + bias_r[k]
        bias_ref[...] = bias_total
        terms = every(recv_v, total - 1, term_send, term_recv)
        terms.wait_send()
        terms.wait_recv()
        lane = lax.broadcasted_iota(jnp.int32, (half_taps, LANES), 1)
        sums = []
        for f in range(fsdp_size):
            piece = recv_v[f].astype(F32)
            for k in range(1, seq_size):
                piece = piece + recv_v[k * fsdp_size + f].astype(F32)
            sums.append(piece)
        for f in range(0, fsdp_size, 2):
            pair = pl.ds(f * groups, 2 * groups)
            fg_ref[:half_taps, pair] = jnp.where(
                lane < groups, sums[f], pltpu.roll(sums[f + 1], groups, 1))
            fg_ref[half_taps:, pair] = jnp.where(
                lane < groups, pltpu.roll(sums[f], groups, 1), sums[f + 1])
    else:
        fg_ref[...] = part_v[...]
        bias_ref[...] = bias_v[...]


def writer(*refs):
    count = len(refs) // 2
    sources, targets, sems = refs[:count], refs[count:2 * count], refs[2 * count]
    copies = [
        pltpu.make_async_copy(a, b, sems.at[i]) for i, (a, b) in enumerate(zip(sources, targets))]
    for copy in copies:
        copy.start()
    for copy in copies:
        copy.wait()


def write_out(*arrays):
    return pl.pallas_call(
        writer,
        out_shape=tuple(pltpu.HBM(a.shape, a.dtype) for a in arrays),
        in_specs=[pl.BlockSpec(memory_space=pltpu.VMEM)] * len(arrays),
        out_specs=(pl.BlockSpec(memory_space=pltpu.HBM),) * len(arrays),
        scratch_shapes=[pltpu.SemaphoreType.DMA((len(arrays),))],
    )(*(pltpu.with_memory_space_constraint(a, pltpu.VMEM) for a in arrays))


def on_device(seq_size, fsdp_size, conv_input, gate, out_grad, filters, skip_bias):
    rows, chans = conv_input.shape
    blocks = chans // LANES
    groups = chans // GS
    width = LF // fsdp_size
    fused = (
        seq_size <= 8 and fsdp_size % 2 == 0
        and 2 * groups == LANES)
    everyone = seq_size * fsdp_size if fused else 1
    fg_shape = (width, fsdp_size * groups) if fused else (groups, LF)
    half_taps = width // 2
    hbm_spec = pl.BlockSpec(memory_space=pltpu.HBM)
    vmem_spec = pl.BlockSpec(memory_space=pltpu.VMEM)
    dma = pltpu.SemaphoreType.DMA
    input_grad, filter_part, bias_part = pl.pallas_call(
        functools.partial(kernel, seq_size, fsdp_size, fused),
        out_shape=(
            jax.ShapeDtypeStruct((rows, chans), BF16),
            jax.ShapeDtypeStruct(fg_shape, F32),
            jax.ShapeDtypeStruct((blocks, LANES), F32),
        ),
        in_specs=[hbm_spec] * 5,
        out_specs=(vmem_spec, vmem_spec, vmem_spec),
        scratch_shapes=[
            pltpu.VMEM((blocks, LANES), F32),
            pltpu.VMEM((rows, chans), BF16),
            pltpu.VMEM((rows, chans), BF16),
            pltpu.VMEM((rows, chans), BF16),
            pltpu.VMEM((rows + LF, chans), BF16),
            pltpu.VMEM((blocks, PER * LF, 2 * LANES), BF16),
            pltpu.VMEM((width, fsdp_size * groups), F32),
            pltpu.VMEM((width, fsdp_size * groups), BF16),
            pltpu.VMEM((LF, LANES), BF16),
            pltpu.VMEM((LANES, LF), F32),
            pltpu.VMEM((groups, LANES), F32),
            pltpu.VMEM((blocks, LANES), F32),
            pltpu.VMEM((2 * groups, LANES), F32),
            pltpu.VMEM((fsdp_size, half_taps, LANES), BF16),
            pltpu.VMEM((everyone, half_taps, LANES), BF16),
            pltpu.VMEM((everyone // fsdp_size if fused else 1, blocks, LANES), F32),
            dma((7,)),
            dma,
            dma((blocks // 2,)),
            dma((fsdp_size,)),
            dma((fsdp_size,)),
            pltpu.SemaphoreType.REGULAR,
            pltpu.SemaphoreType.REGULAR,
            pltpu.SemaphoreType.REGULAR,
            dma,
            dma,
            dma,
            dma,
        ],
        compiler_params=pltpu.CompilerParams(
            collective_id=0, has_side_effects=True, vmem_limit_bytes=VMEM_GRANT),
    )(*(pltpu.with_memory_space_constraint(a, pltpu.HBM) for a in (
        conv_input, gate, out_grad, filters.T, skip_bias.reshape(blocks, LANES))))
    if fused:
        input_grad, filter_part, bias_part = write_out(input_grad, filter_part, bias_part)
        return input_grad, filter_part.T, bias_part.reshape(chans)
    spread = lax.all_to_all(
        filter_part, "fsdp", split_axis=1, concat_axis=0, tiled=True)
    filter_grad, bias_grad = lax.psum((spread, bias_part.reshape(chans)), "seq")
    return input_grad, filter_grad, bias_grad


def solution(mesh):
    placed = (P("seq", "fsdp"), P("seq", "fsdp"), P("seq", "fsdp"), P(None, "fsdp"), P("fsdp"))
    return jax.shard_map(
        functools.partial(on_device, mesh.shape["seq"], mesh.shape["fsdp"]),
        mesh=mesh,
        in_specs=placed,
        out_specs=(P("seq", "fsdp"), P(None, "fsdp"), P("fsdp")),
        check_vma=False,
    )
```

```python
import functools

import jax
import jax.numpy as jnp
from jax import lax
from jax.experimental import pallas as pl
from jax.experimental.pallas import tpu as pltpu
from jax.sharding import PartitionSpec as P

GS = 16
VMEM_GRANT = 105 << 19
LF = 128
LANES = 128
PER = LANES // GS
MESH = pl.DeviceIdType.MESH
F32 = jnp.float32
BF16 = jnp.bfloat16


def kernel(
    seq_size, fsdp_size, fused,
    x_hbm, gate_hbm, og_hbm, filt_hbm, skip_hbm,
    ig_ref, fg_ref, bias_ref,
    skip_ref, x_v, gate_v, og_v, sg_v, toep_v, taps_r, taps_v, part_v, bias_v,
    pack_v, send_v, recv_v, bias_r,
    load_sem, halo_send, halo_recv, tap_send, tap_recv, row_sem, late_sem, all_sem, term_send, term_recv, bias_send, bias_recv,
):
    rows, chans = x_v.shape
    blocks = chans // LANES
    pairs = rows // (2 * LF)
    groups = chans // GS
    me_s = lax.axis_index("seq")
    me_f = lax.axis_index("fsdp")

    width = LF // fsdp_size
    sharing = LANES // groups

    def tap_lanes(owner):
        return pl.ds(pl.multiple_of(lax.div(owner, sharing) * LANES, LANES), LANES)

    def tap_rows(source):
        return pl.ds(pl.multiple_of(source * width, 8), width)

    rim = pl.ds(0, LF)
    rest = pl.ds(LF, rows - LF)
    loads = [
        pltpu.make_async_copy(og_hbm.at[rim], og_v.at[rim], load_sem.at[0]),
        pltpu.make_async_copy(gate_hbm.at[rim], gate_v.at[rim], load_sem.at[1]),
        pltpu.make_async_copy(og_hbm.at[rest], og_v.at[rest], load_sem.at[2]),
        pltpu.make_async_copy(gate_hbm.at[rest], gate_v.at[rest], load_sem.at[3]),
        pltpu.make_async_copy(x_hbm, x_v, load_sem.at[4]),
        pltpu.make_async_copy(
            filt_hbm.at[:, tap_lanes(me_f)], taps_r.at[tap_rows(me_f)], load_sem.at[5]),
        pltpu.make_async_copy(skip_hbm, skip_ref, load_sem.at[6]),
    ]
    barrier = pltpu.get_barrier_semaphore()
    def greet(semaphore, first, end):
        def step(other, c):
            o_s, o_f = lax.div(other, fsdp_size), lax.rem(other, fsdp_size)
            pl.semaphore_signal(
                semaphore, inc=1, device_id=(o_s, o_f), device_id_type=MESH)
            return c

        lax.fori_loop(first, end, step, 0)

    if fused:
        me = me_s * fsdp_size + me_f
        total = seq_size * fsdp_size
        row = me_s * fsdp_size
        row_end = row + fsdp_size

        def greet_column(semaphore, first, end):
            def step(o_s, c):
                pl.semaphore_signal(semaphore, inc=1, device_id=(o_s, me_f), device_id_type=MESH)
                return c

            lax.fori_loop(first, end, step, 0)

        greet_column(barrier, me_s + 1, seq_size)
        greet(barrier, me + 1, row_end)
    else:
        for d in range(1, fsdp_size):
            pl.semaphore_signal(
                barrier, inc=1, device_id=(me_s, lax.rem(me_f + d, fsdp_size)),
                device_id_type=MESH)

        @pl.when(me_s > 0)
        def _():
            pl.semaphore_signal(
                barrier, inc=1, device_id=(me_s - 1, me_f), device_id_type=MESH)

        @pl.when(me_s < seq_size - 1)
        def _():
            pl.semaphore_signal(
                barrier, inc=1, device_id=(me_s + 1, me_f), device_id_type=MESH)

    for load in loads:
        load.start()
    loads[0].wait()
    loads[1].wait()
    sg_v[rim, :] = (og_v[rim, :].astype(F32) * gate_v[rim, :].astype(F32)).astype(BF16)

    if fused:
        @pl.when(me_s + me_f > 0)
        def _():
            pl.semaphore_wait(barrier, me_s + me_f)
    else:
        pl.semaphore_wait(barrier, fsdp_size - 1)

        @pl.when(me_s > 0)
        def _():
            pl.semaphore_wait(barrier, 1)

        @pl.when(me_s < seq_size - 1)
        def _():
            pl.semaphore_wait(barrier, 1)

    def lanes_of(b):
        return pl.ds(pl.multiple_of(b * LANES, LANES), LANES)

    def halo_copy(target, first, end):
        lanes = pl.ds(first * LANES, (end - first) * LANES)
        return pltpu.make_async_remote_copy(
            src_ref=sg_v.at[rim, lanes], dst_ref=sg_v.at[pl.ds(rows, LF), lanes],
            send_sem=halo_send, recv_sem=halo_recv.at[first // 2],
            device_id=(target, me_f), device_id_type=MESH)

    @pl.when(me_s > 0)
    def _():
        for b in range(0, blocks, 2):
            halo_copy(me_s - 1, b, b + 2).start()

    def tap_copy(other):
        return pltpu.make_async_remote_copy(
            src_ref=filt_hbm.at[:, tap_lanes(other)],
            dst_ref=taps_r.at[tap_rows(me_f)],
            send_sem=tap_send.at[other], recv_sem=tap_recv.at[me_f],
            device_id=(me_s, other), device_id_type=MESH)

    def tap_arrival(d):
        other = lax.rem(me_f + d, fsdp_size)
        return pltpu.make_async_remote_copy(
            src_ref=filt_hbm.at[:, tap_lanes(other)],
            dst_ref=taps_r.at[tap_rows(other)],
            send_sem=tap_send.at[other], recv_sem=tap_recv.at[other],
            device_id=(me_s, other), device_id_type=MESH)

    def send_taps(first, end):
        def step(other, c):
            tap_copy(other).start()
            return c

        lax.fori_loop(first, end, step, 0)

    if fused:
        greet(row_sem, row, me)
        greet_column(late_sem, 0, me_s)
    else:
        send_taps(me_f + 1, fsdp_size)
    send_taps(0, me_f)

    @pl.when(me_s == seq_size - 1)
    def _():
        sg_v[pl.ds(rows, LF), :] = jnp.zeros((LF, chans), BF16)

    for load in loads[2:5]:
        load.wait()

    def scale(b, c):
        lanes = lanes_of(b)
        new = (og_v[rest, lanes].astype(F32) * gate_v[rest, lanes].astype(F32)).astype(BF16)
        sg_v[rest, lanes] = new
        terms = jnp.sum(new.astype(F32) * x_v[rest, lanes].astype(F32), axis=0, keepdims=True)
        terms = terms + jnp.sum(
            sg_v[rim, lanes].astype(F32) * x_v[rim, lanes].astype(F32), axis=0, keepdims=True)
        bias_v[pl.ds(b, 1), :] = terms
        return c

    lax.fori_loop(0, blocks, scale, 0, unroll=2)

    if fused:
        def bias_copy(o_s):
            return pltpu.make_async_remote_copy(
                src_ref=bias_v, dst_ref=bias_r.at[me_s], send_sem=bias_send, recv_sem=bias_recv,
                device_id=(o_s, me_f), device_id_type=MESH)

        def send_bias(first, end):
            def step(o_s, c):
                bias_copy(o_s).start()
                return c

            lax.fori_loop(first, end, step, 0)

        send_bias(0, me_s)

    row_at = lax.broadcasted_iota(jnp.int32, (LF, LANES), 0)
    lane_at = lax.broadcasted_iota(jnp.int32, (LF, LANES), 1)
    above = lane_at >= row_at

    def windows(p, lanes):
        at = 2 * LF * p
        return jnp.concatenate(
            [sg_v[at:at + 2 * LF, lanes], sg_v[at + LF:at + 3 * LF, lanes]], axis=1)

    def split_groups(both):
        lane = lax.broadcasted_iota(jnp.int32, both.shape, 1)
        owner = lax.rem(lax.div(lane, GS), PER)
        return jnp.concatenate(
            [both * (owner == g).astype(F32).astype(BF16) for g in range(PER)], axis=0)

    def products(left, right):
        return lax.dot_general(
            split_groups(left), right, (((1,), (1,)), ((), ())), preferred_element_type=F32)

    def fold(wrapped):
        parts = [wrapped[:8]] + [
            pltpu.roll(wrapped[8 * k:8 * k + 8], LANES - 8 * k, 1) for k in range(1, LF // 8)]
        while len(parts) > 1:
            parts = [one + two for one, two in zip(parts[::2], parts[1::2])]
        return parts[0]

    sub = lax.broadcasted_iota(jnp.int32, (8, LANES), 0)

    def diagonals(wholes):
        for bit in (2, 1, 0):
            step = 1 << bit
            odd = lax.rem(lax.div(sub, step), 2) == 1
            wholes = [
                jnp.where(odd, pltpu.roll(wholes[i + step], step, 0), wholes[i])
                + pltpu.roll(
                    jnp.where(odd, wholes[i + step], pltpu.roll(wholes[i], 8 - step, 0)),
                    LANES - step, 1)
                for i in range(step)]
        return wholes[0]

    def tiles(ref, lanes, span, count):
        return jnp.concatenate([ref[at:at + span, lanes] for at in range(0, count * LF, LF)], axis=1)

    def correlate(b):
        lanes = lanes_of(b)
        prod = products(
            tiles(x_v, lanes, LF, rows // LF), tiles(sg_v, lanes, 2 * LF, rows // LF))
        wholes = []
        for g in range(PER):
            one = prod[g * LF:(g + 1) * LF]
            wholes.append(fold(jnp.where(above, one[:, :LANES], one[:, LANES:])))
        part_v[pl.ds(pl.multiple_of(b * PER, PER), PER), :] = diagonals(wholes)

    def correlate_own(b):
        lanes = lanes_of(b)
        last = jnp.concatenate(
            [sg_v[rows - LF:rows, lanes], jnp.zeros((LF, LANES), BF16)], axis=0)
        prod = products(
            tiles(x_v, lanes, LF, rows // LF),
            jnp.concatenate([tiles(sg_v, lanes, 2 * LF, rows // LF - 1), last], axis=1))
        wholes = []
        for g in range(PER):
            one = prod[g * LF:(g + 1) * LF]
            wholes.append(fold(jnp.where(above, one[:, :LANES], one[:, LANES:])))
        part_v[b * PER:(b + 1) * PER, :] = diagonals(wholes)

    def correlate_next(b):
        lanes = lanes_of(b)
        prod = products(x_v[rows - LF:rows, lanes], sg_v[rows:rows + LF, lanes])
        wholes = []
        for g in range(PER):
            one = prod[g * LF:(g + 1) * LF]
            wholes.append(fold(jnp.where(above, jnp.zeros_like(one), one)))
        return diagonals(wholes)

    def halo_arrival(i):
        @pl.when(me_s < seq_size - 1)
        def _():
            lanes = pl.ds(pl.multiple_of(i * 2 * LANES, 2 * LANES), 2 * LANES)
            pltpu.make_async_remote_copy(
                src_ref=sg_v.at[rim, lanes], dst_ref=sg_v.at[pl.ds(rows, LF), lanes],
                send_sem=halo_send, recv_sem=halo_recv.at[i],
                device_id=(me_s + 1, me_f), device_id_type=MESH).wait_recv()

    def correlate_two(i, c):
        halo_arrival(i)
        correlate(2 * i)
        correlate(2 * i + 1)
        return c

    def build(b):
        first = lax.rem(me_f, sharing) * groups + b * PER
        taps = taps_v[pl.ds(pl.multiple_of(first, PER), PER), :]
        for g in range(PER):
            band = pltpu.roll(
                jnp.broadcast_to(taps[g:g + 1], (LF, LANES)), 0, 1, stride=1, stride_axis=0)
            zero = jnp.zeros_like(band)
            toep_v[b, g * LF:(g + 1) * LF, :LANES] = jnp.where(above, band, zero).astype(BF16)
            toep_v[b, g * LF:(g + 1) * LF, LANES:] = jnp.where(above, zero, band).astype(BF16)

    def conv(b, p):
        lanes = lanes_of(b)
        at = 2 * LF * p
        prod = jnp.dot(toep_v[b], windows(p, lanes), preferred_element_type=F32)
        owner = lax.div(lax.broadcasted_iota(jnp.int32, (LF, 2 * LANES), 1), GS)
        owner = lax.rem(owner, PER)
        out = prod[:LF]
        for g in range(1, PER):
            out = jnp.where(owner == g, prod[g * LF:(g + 1) * LF], out)
        skip = skip_ref[pl.ds(b, 1), :]
        for half in range(2):
            here = slice(at + half * LF, at + (half + 1) * LF)
            direct = skip * sg_v[here, lanes].astype(F32)
            ig_ref[here, lanes] = (
                out[:, half * LANES:(half + 1) * LANES] + direct).astype(BF16)

    correlate_own(blocks - 2)
    correlate_own(blocks - 1)
    if fused:
        @pl.when(me_f < fsdp_size - 1)
        def _():
            pl.semaphore_wait(row_sem, fsdp_size - 1 - me_f)

        send_taps(me_f + 1, fsdp_size)
    early_pairs = (blocks // 2 - 1) // 2 + 1

    def correlate_pairs(i, c):
        correlate_two(i, c)
        if fused:
            @pl.when(i == early_pairs - 1)
            def _():
                @pl.when(me_s < seq_size - 1)
                def _():
                    pl.semaphore_wait(late_sem, seq_size - 1 - me_s)

                greet(all_sem, row, me)
                greet(all_sem, me + 1, row_end)
                send_bias(me_s + 1, seq_size)

        return c

    lax.fori_loop(0, blocks // 2 - 1, correlate_pairs, 0)

    halo_arrival(blocks // 2 - 1)
    here = pl.ds(groups - 2 * PER, 2 * PER)
    part_v[here, :] = part_v[here, :] + jnp.concatenate(
        [correlate_next(blocks - 2), correlate_next(blocks - 1)], axis=0)

    if fused:
        half_taps = width // 2
        pack_v[:groups, :] = part_v[...]
        pack_v[groups:, :] = pltpu.roll(part_v[...], LANES - half_taps, 1)
        turned = pack_v[...].T.astype(BF16)
        for f in range(fsdp_size):
            send_v[f] = turned[f * width:f * width + half_taps]
        recv_v[me] = send_v[me_f]
        pl.semaphore_wait(all_sem, fsdp_size - 1)

        def send_terms(other, c):
            o_s, o_f = lax.div(other, fsdp_size), lax.rem(other, fsdp_size)
            pltpu.make_async_remote_copy(
                src_ref=send_v.at[o_f], dst_ref=recv_v.at[me],
                send_sem=term_send, recv_sem=term_recv,
                device_id=(o_s, o_f), device_id_type=MESH).start()
            return c

        lax.fori_loop(0, me, send_terms, 0)
        lax.fori_loop(me + 1, total, send_terms, 0)

    loads[5].wait()
    loads[6].wait()
    for d in range(1, fsdp_size):
        tap_arrival(d).wait_recv()
    taps_v[...] = taps_r[...].T

    def build_conv(b, c):
        build(b)
        for p in range(pairs):
            conv(b, p)
        return c

    lax.fori_loop(0, blocks, build_conv, 0, unroll=2)

    for d in range(1, fsdp_size):
        tap_copy(lax.rem(me_f + d, fsdp_size)).wait_send()

    @pl.when(me_s > 0)
    def _():
        halo_copy(me_s - 1, 0, blocks).wait_send()

    if fused:
        def every(ref, slots, send_sem, recv_sem):
            span = ref.at[pl.ds(0, slots)]
            return pltpu.make_async_remote_copy(
                src_ref=span, dst_ref=span, send_sem=send_sem, recv_sem=recv_sem,
                device_id=(lax.rem(me_s + 1, seq_size), me_f), device_id_type=MESH)

        biases = every(bias_r, seq_size - 1, bias_send, bias_recv)
        biases.wait_send()
        biases.wait_recv()
        bias_r[me_s] = bias_v[...]
        bias_total = bias_r[0]
        for k in range(1, seq_size):
            bias_total = bias_total + bias_r[k]
        bias_ref[...] = bias_total
        terms = every(recv_v, total - 1, term_send, term_recv)
        terms.wait_send()
        terms.wait_recv()
        lane = lax.broadcasted_iota(jnp.int32, (half_taps, LANES), 1)
        sums = []
        for f in range(fsdp_size):
            piece = recv_v[f].astype(F32)
            for k in range(1, seq_size):
                piece = piece + recv_v[k * fsdp_size + f].astype(F32)
            sums.append(piece)
        for f in range(0, fsdp_size, 2):
            pair = pl.ds(f * groups, 2 * groups)
            fg_ref[:half_taps, pair] = jnp.where(
                lane < groups, sums[f], pltpu.roll(sums[f + 1], groups, 1))
            fg_ref[half_taps:, pair] = jnp.where(
                lane < groups, pltpu.roll(sums[f], groups, 1), sums[f + 1])
    else:
        fg_ref[...] = part_v[...]
        bias_ref[...] = bias_v[...]


def writer(*refs):
    count = len(refs) // 2
    sources, targets, sems = refs[:count], refs[count:2 * count], refs[2 * count]
    copies = [
        pltpu.make_async_copy(a, b, sems.at[i]) for i, (a, b) in enumerate(zip(sources, targets))]
    for copy in copies:
        copy.start()
    for copy in copies:
        copy.wait()


def write_out(*arrays):
    return pl.pallas_call(
        writer,
        out_shape=tuple(pltpu.HBM(a.shape, a.dtype) for a in arrays),
        in_specs=[pl.BlockSpec(memory_space=pltpu.VMEM)] * len(arrays),
        out_specs=(pl.BlockSpec(memory_space=pltpu.HBM),) * len(arrays),
        scratch_shapes=[pltpu.SemaphoreType.DMA((len(arrays),))],
    )(*(pltpu.with_memory_space_constraint(a, pltpu.VMEM) for a in arrays))


def on_device(seq_size, fsdp_size, conv_input, gate, out_grad, filters, skip_bias):
    rows, chans = conv_input.shape
    blocks = chans // LANES
    groups = chans // GS
    width = LF // fsdp_size
    fused = (
        seq_size <= 8 and fsdp_size % 2 == 0
        and 2 * groups == LANES)
    everyone = seq_size * fsdp_size if fused else 1
    fg_shape = (width, fsdp_size * groups) if fused else (groups, LF)
    half_taps = width // 2
    hbm_spec = pl.BlockSpec(memory_space=pltpu.HBM)
    vmem_spec = pl.BlockSpec(memory_space=pltpu.VMEM)
    dma = pltpu.SemaphoreType.DMA
    input_grad, filter_part, bias_part = pl.pallas_call(
        functools.partial(kernel, seq_size, fsdp_size, fused),
        out_shape=(
            jax.ShapeDtypeStruct((rows, chans), BF16),
            jax.ShapeDtypeStruct(fg_shape, F32),
            jax.ShapeDtypeStruct((blocks, LANES), F32),
        ),
        in_specs=[hbm_spec] * 5,
        out_specs=(vmem_spec, vmem_spec, vmem_spec),
        scratch_shapes=[
            pltpu.VMEM((blocks, LANES), F32),
            pltpu.VMEM((rows, chans), BF16),
            pltpu.VMEM((rows, chans), BF16),
            pltpu.VMEM((rows, chans), BF16),
            pltpu.VMEM((rows + LF, chans), BF16),
            pltpu.VMEM((blocks, PER * LF, 2 * LANES), BF16),
            pltpu.VMEM((LF, LANES), F32),
            pltpu.VMEM((LANES, LF), F32),
            pltpu.VMEM((groups, LANES), F32),
            pltpu.VMEM((blocks, LANES), F32),
            pltpu.VMEM((2 * groups, LANES), F32),
            pltpu.VMEM((fsdp_size, half_taps, LANES), BF16),
            pltpu.VMEM((everyone, half_taps, LANES), BF16),
            pltpu.VMEM((everyone // fsdp_size if fused else 1, blocks, LANES), F32),
            dma((7,)),
            dma,
            dma((blocks // 2,)),
            dma((fsdp_size,)),
            dma((fsdp_size,)),
            pltpu.SemaphoreType.REGULAR,
            pltpu.SemaphoreType.REGULAR,
            pltpu.SemaphoreType.REGULAR,
            dma,
            dma,
            dma,
            dma,
        ],
        compiler_params=pltpu.CompilerParams(
            collective_id=0, has_side_effects=True, vmem_limit_bytes=VMEM_GRANT),
    )(*(pltpu.with_memory_space_constraint(a, pltpu.HBM) for a in (
        conv_input, gate, out_grad, filters.T, skip_bias.reshape(blocks, LANES))))
    if fused:
        input_grad, filter_part, bias_part = write_out(input_grad, filter_part, bias_part)
        return input_grad, filter_part.T, bias_part.reshape(chans)
    spread = lax.all_to_all(
        filter_part, "fsdp", split_axis=1, concat_axis=0, tiled=True)
    filter_grad, bias_grad = lax.psum((spread, bias_part.reshape(chans)), "seq")
    return input_grad, filter_grad, bias_grad


def solution(mesh):
    placed = (P("seq", "fsdp"), P("seq", "fsdp"), P("seq", "fsdp"), P(None, "fsdp"), P("fsdp"))
    return jax.shard_map(
        functools.partial(on_device, mesh.shape["seq"], mesh.shape["fsdp"]),
        mesh=mesh,
        in_specs=placed,
        out_specs=(P("seq", "fsdp"), P(None, "fsdp"), P("fsdp")),
        check_vma=False,
    )
```
